128 devices in a mesh: corpus: 16 (over z, y), fsdp: 2 (over core), tensor: 4 (over x).
Axes of the slice: x: 4, y: 4, z: 4, core: 2. Of those that a mesh axis runs over, the one named last changes fastest.
Arguments:
- queries_in: bfloat16 [4096, 4096], P(('corpus', 'fsdp')), may hold values from -6 to 6
- head_weight: bfloat16 [4096, 4096], P('fsdp', 'tensor'), may hold values from -0.09375 to 0.09375
- passages: bfloat16 [16384, 4096], P('corpus', 'tensor'), may hold values from -0.15625 to 0.15625
- teacher: float32 [4096, 4, 32], P(('corpus', 'fsdp')), may hold values from -250 to 400
- cand_block: int32 [4096, 4], P(('corpus', 'fsdp')), may hold values from 0 to 127, all different within a row; in each aligned block of 128 rows (0 to 127, 128 to 255, ...) at most 6 rows name the same one
- cand_offset: int32 [4096, 4, 32], P(('corpus', 'fsdp')), may hold values from 0 to 127, as said below
- block_slot: int32 [128], replicated, may hold values from 0 to 127, each once
Outputs:
- kl_loss: float32 [4096], P(('corpus', 'fsdp'))
- head_grad: float32 [4096, 4096], P('fsdp', 'tensor')
The draws below stay inside these ranges and needn't reach their ends.
Inputs may be any that keep to these rules, and one draw needn't show every extreme that they name: `cand_block`: in the rows of one device no block id appears more than 6 times, and some block id appears exactly 6 times there; the 4 ids of one query differ. `cand_offset`: the 32 offsets of one query in one block differ. `block_slot`: each storage position is taken by exactly one block.
All inputs are finite; a program needn't handle non-finite values.
Results may differ from the reference program's by a relative error of at most 0.012.
The reference program's roundings to bfloat16 on the way (of `query`, `dscore`, `block_part` and `query_grad`) count: a program that leaves them out, or rounds other values in their place, can miss the bound.
Values may be sent and summed in bfloat16 or wider, within the bound.
A program may use at most 128 MiB of HBM per device.

```python
import math
import jax
import jax.numpy as jnp
import numpy as np
from jax import lax

D = 4096
QDEV = 128
G = 4
OFFS = 32
ROWS = 128
NB = 128
MOSTB = 6
Q = 4096


def draw_passages(key, part):
    sigma = 0.04 / D ** 0.5
    first, second = jax.random.split(key, 2)
    base = jax.random.truncated_normal(first, -4.0, 4.0, (NB * ROWS, D), jnp.float32)
    spread = jnp.exp(jax.random.uniform(second, (NB * ROWS, 1), jnp.float32, -0.7, 0.7))
    return (sigma * spread * base).astype(jnp.bfloat16)


def draw_teacher(key, part):
    first, second = jax.random.split(key, 2)
    base = jax.random.truncated_normal(first, -4.0, 4.0, (Q, G, OFFS), jnp.float32)
    spread = jnp.exp(jax.random.uniform(second, (Q, 1, 1), jnp.float32, -0.7, 0.7))
    return 2.0 * spread * base


def draw_cand_offset(key, part):
    raw_keys = jax.random.randint(key, (Q, G, ROWS), 0, 1 << 20, jnp.int32)
    keyed = raw_keys * ROWS + lax.broadcasted_iota(jnp.int32, (Q, G, ROWS), 2)
    ordering = jnp.argsort(keyed, axis=2, stable=True)
    return ordering[:, :, :OFFS].astype(jnp.int32)


def levels(rng, shape, cuts, low, high):
    def one(axis_at, blocks):
        draws = jax.random.uniform(jax.random.fold_in(jax.random.fold_in(rng, 6), axis_at), (blocks,), jnp.float32, low / len(cuts), high / len(cuts))
        return jnp.repeat(jnp.exp(draws), shape[axis_at] // blocks).reshape((-1,) + (1,) * (len(shape) - axis_at - 1))

    level = one(*cuts[0])
    for cut in cuts[1:]:
        level = level * one(*cut)
    return level


def deal_out(key, own, number, rows, number_of, top, limit, skew):
    sequence = jax.random.permutation(key, number_of)
    crowded, ordinary = load_shares(number_of, rows * top, limit, skew, True), load_shares(number_of, rows * top, limit, skew, False)
    places = jnp.arange(number_of)

    def named(tallies, turn):
        used = int((tallies > 0).sum())
        fixed = max(1, used // 4)
        moved = fixed + (places - fixed + turn * (used - fixed)) % max(1, number_of - fixed)
        return jnp.zeros((number_of,), jnp.int32).at[sequence[jnp.where(places < fixed, places, moved)]].set(jnp.asarray(tallies, jnp.int32))

    tallies = jnp.where(number % 4 == 0, named(crowded, number // 4), named(ordinary, number - number // 4 - 1))
    mixed = jax.random.permutation(jax.random.fold_in(own, 3), number_of)
    giver, receiver = mixed[0:number_of // 2 * 2:2], mixed[1:number_of // 2 * 2:2]
    room = jnp.minimum(tallies[giver] - 1, limit - tallies[receiver]) // 2
    room = jnp.where((giver == sequence[0]) | (receiver == sequence[0]) | (tallies[receiver] == 0), 0, jnp.maximum(room, 0))
    moved = jax.random.randint(jax.random.fold_in(own, 4), (number_of // 2,), 0, 1 << 20) % (room + 1)
    tallies = tallies.at[giver].add(-moved).at[receiver].add(moved)
    labels = jnp.searchsorted(jnp.cumsum(tallies), jnp.arange(rows * top), side="right").astype(jnp.int32)
    grid = labels.reshape(top, rows).T
    grid = grid[jax.random.permutation(jax.random.fold_in(own, 1), rows)]
    turn = jax.random.randint(jax.random.fold_in(own, 2), (rows, 1), 0, top)
    return jnp.take_along_axis(grid, (jnp.arange(top)[None, :] + turn) % top, axis=1)


def load_shares(count, total, reach, slope, full):
    portions = [(1 << 20) // math.isqrt(grade ** slope) + 1 for grade in range(1, count + 1)]
    largest = reach if full else min(reach, max(-(-total // count), total * portions[0] // sum(portions)))
    least = 1 if total - largest >= count - 1 else 0
    holding, rest = [largest] + [least] * (count - 1), total - largest - least * (count - 1)
    while rest > 0:
        free = [i for i in range(1, count) if holding[i] < largest] or [i for i in range(1, count) if holding[i] < reach]
        mass, budget = sum([portions[i] for i in free]), rest
        for i in free:
            more = min(reach - holding[i], max(1, budget * portions[i] // mass), rest)
            holding[i] = holding[i] + more
            rest = rest - more
    return np.array(holding)


def gaussian(stream_key, shape, deviation, reach, cuts=(), kind=jnp.bfloat16):
    result = deviation * jax.random.normal(stream_key, shape, jnp.float32)
    if cuts:
        result = result * levels(stream_key, shape, cuts, -0.22, 0.18)
    return jnp.clip(result, -reach, reach).astype(kind)


def setup_inputs(seed: int = 0) -> dict:
    seeds = jax.random.split(jax.random.key(seed), 8)
    queries_in = gaussian(seeds[0], (Q, D), 1.0, 6.0, ((0, 32),))
    head_weight = gaussian(seeds[1], (D, D), D ** -0.5, 0.09375, ((0, 2), (1, 4)))
    passages = draw_passages(jax.random.fold_in(seeds[7], 71), 0)
    teacher = draw_teacher(jax.random.fold_in(seeds[7], 71), 0)
    cand_block_keys = jax.random.split(jax.random.fold_in(seeds[4], 1), Q // QDEV)
    cand_block_turns = jax.random.permutation(jax.random.fold_in(seeds[4], 3), Q // QDEV)
    cand_block = jax.vmap(lambda own, number: deal_out(jax.random.fold_in(seeds[4], 2), own, number, QDEV, NB, G, MOSTB, 2))(cand_block_keys, cand_block_turns).reshape((Q, G))
    cand_offset = draw_cand_offset(jax.random.fold_in(seeds[7], 71), 0)
    block_slot = jax.random.permutation(seeds[6], NB).astype(jnp.int32)
    return dict(queries_in=queries_in, head_weight=head_weight, passages=passages, teacher=teacher, cand_block=cand_block, cand_offset=cand_offset, block_slot=block_slot)


def reference(queries_in, head_weight, passages, teacher, cand_block, cand_offset, block_slot):
    query = jnp.dot(queries_in, head_weight, preferred_element_type=jnp.float32).astype(jnp.bfloat16)
    cand_rows = (block_slot[cand_block] * ROWS).astype(jnp.int32)[:, :, None] + cand_offset.astype(jnp.int32)
    block_count = query.shape[0] // 16

    def per_block(inputs_block):
        query_block, rows_block, teacher_block = inputs_block
        embedded = passages[rows_block].astype(jnp.float32)
        student = 50.0 * jnp.einsum("id,igkd->igk", query_block.astype(jnp.float32), embedded)
        log_student = student - jax.nn.logsumexp(student, axis=(1, 2), keepdims=True)
        log_teacher = teacher_block - jax.nn.logsumexp(teacher_block, axis=(1, 2), keepdims=True)
        prob_teacher = jnp.exp(log_teacher)
        kl_part = jnp.sum(prob_teacher * (log_teacher - log_student), axis=(1, 2))
        dscore = (50.0 * (jnp.exp(log_student) - prob_teacher)).astype(jnp.bfloat16)
        block_part = jnp.einsum("igk,igkd->igd", dscore.astype(jnp.float32), embedded).astype(jnp.bfloat16)
        query_grad = jnp.sum(block_part.astype(jnp.float32), axis=1).astype(jnp.bfloat16)
        return kl_part, query_grad

    kl_loss, query_grad = lax.map(
        per_block,
        (query.reshape(block_count, 16, D), cand_rows.reshape(block_count, 16, G, OFFS),
         teacher.reshape(block_count, 16, G, OFFS)))
    query_grad = query_grad.reshape(-1, D)
    head_grad = lax.dot_general(queries_in, query_grad, (((0,), (0,)), ((), ())),
                                preferred_element_type=jnp.float32)
    return kl_loss.reshape(-1), head_grad
```

```python
import functools
import jax
import jax.numpy as jnp
from jax import lax
from jax.experimental import pallas as pl
from jax.experimental.pallas import tpu as pltpu
from jax.sharding import PartitionSpec as P

BF = jnp.bfloat16
F32 = jnp.float32
I32 = jnp.int32
ROWS = 128
CAP = 6
SIDE = 4
SLOTS = 48
ALL = 768
LANES = 128
MESH = pl.DeviceIdType.MESH


def dot(a, b, dims=((1,), (0,))):
    return lax.dot_general(a, b, (dims, ((), ())), preferred_element_type=F32)


def lane_pick(values, index):
    return jnp.take_along_axis(values, index, axis=1)


def step_kernel(x_hbm, w_hbm, p_hbm, teacher_ref, offs_ref, cand_ref, bslot_ref,
                kl_ref, hg_ref,
                xcat, xt, w, p, part_own, part_send, part_recv, q,
                pmt, pm, r, rt, inv,
                qs, qr, ss, sr, s3, st, ds, dr, dexp, ps, pr, qg2,
                gsend, grecv, gown, hsend, hrecv,
                loc_sem, fs_send, fs_recv, aa_send, aa_recv, te_send, te_recv,
                ar_send, ar_recv):
    c = lax.axis_index("corpus")
    f = lax.axis_index("fsdp")
    t = lax.axis_index("tensor")
    z = lax.div(c, SIDE)
    y = lax.rem(c, SIDE)

    def load(src, dst, k):
        return pltpu.make_async_copy(src, dst, loc_sem.at[k])

    own_cols = pl.ds(pl.multiple_of(f * 2048, 2048), 2048)
    other_cols = pl.ds(pl.multiple_of((1 - f) * 2048, 2048), 2048)
    load_x = load(x_hbm.at[:, own_cols], xcat.at[pl.ds(0, 128), :], 0)
    load_w = load(w_hbm, w, 1)
    load_p = load(p_hbm, p, 2)
    load_x.start()
    load_w.start()
    load_p.start()

    barrier = pltpu.get_barrier_semaphore()

    def peer(dz, dy):
        return lax.rem(z + dz, SIDE) * SIDE + lax.rem(y + dy, SIDE)

    def source(dz, dy):
        return lax.rem(z + SIDE - dz, SIDE) * SIDE + lax.rem(y + SIDE - dy, SIDE)

    pl.semaphore_signal(barrier, inc=1, device_id={"fsdp": 1 - f}, device_id_type=MESH)

    @pl.loop(1, 4)
    def _(i):
        pl.semaphore_signal(
            barrier, inc=1, device_id={"tensor": lax.rem(t + i, 4)}, device_id_type=MESH)

    @pl.loop(1, 16)
    def _(i):
        pl.semaphore_signal(
            barrier, inc=1, device_id={"corpus": peer(lax.div(i, SIDE), lax.rem(i, SIDE))},
            device_id_type=MESH)

    pl.semaphore_wait(barrier, 19)

    swap_x = pltpu.make_async_remote_copy(
        src_ref=x_hbm.at[:, other_cols], dst_ref=xcat.at[pl.ds(128, 128), :],
        send_sem=fs_send.at[0], recv_sem=fs_recv.at[0],
        device_id={"fsdp": 1 - f}, device_id_type=MESH)
    swap_x.start()

    lane = lax.broadcasted_iota(I32, (128, LANES), 1)
    row = lax.broadcasted_iota(I32, (128, LANES), 0)
    slot_row = bslot_ref[...].astype(F32)
    hits = jnp.zeros((128, LANES), F32)
    slots = []
    for g in range(4):
        named = cand_ref[:, g:g + 1] == lane
        slot = jnp.sum(jnp.where(named, slot_row, 0.0), axis=1, keepdims=True).astype(I32)
        slots.append(slot)
        hits = hits + jnp.where(slot == lane, 1.0, 0.0)
    earlier = jnp.where(lane < row, 1.0, 0.0).astype(BF)
    before = dot(earlier, hits.astype(BF))
    place_lane = lax.broadcasted_iota(I32, (128, ALL), 1)
    total = jnp.zeros((128, ALL), F32)
    for g in range(4):
        rank = jnp.sum(jnp.where(slots[g] == lane, before, 0.0), axis=1, keepdims=True).astype(I32)
        place = (slots[g] >> 3) * SLOTS + rank * 8 + (slots[g] & 7)
        one = jnp.where(place == place_lane, 1.0, 0.0)
        total = total + one
        pmt[g, :, :] = one.astype(BF)
        pm[:, g * 128:(g + 1) * 128] = one.T.astype(BF)
    rt[...] = total.astype(BF)
    r[...] = total.T.astype(BF)

    load_x.wait()
    load_w.wait()

    @pl.loop(0, 4)
    def _(n):
        cols = pl.ds(pl.multiple_of(n * 256, 256), 256)
        part_own[:, cols] = dot(xcat[0:128, :], w[:, cols])

    swap_x.wait_recv()

    @pl.loop(0, 4)
    def _(n):
        cols = pl.ds(pl.multiple_of(n * 256, 256), 256)
        part_send[:, cols] = dot(xcat[128:256, :], w[:, cols])

    swap_part = pltpu.make_async_remote_copy(
        src_ref=part_send, dst_ref=part_recv,
        send_sem=fs_send.at[1], recv_sem=fs_recv.at[1],
        device_id={"fsdp": 1 - f}, device_id_type=MESH)
    swap_part.start()
    swap_part.wait_recv()
    q[...] = (part_own[...] + part_recv[...]).astype(BF)

    def out_copy(src, dst, chan, dz, dy):
        to = peer(dz, dy)
        return pltpu.make_async_remote_copy(
            src_ref=src.at[pl.ds(pl.multiple_of(to * SLOTS, 16), SLOTS), :],
            dst_ref=dst.at[pl.ds(pl.multiple_of(c * SLOTS, 16), SLOTS), :],
            send_sem=aa_send.at[chan, dz * SIDE + dy], recv_sem=aa_recv.at[chan, dz * SIDE + dy],
            device_id={"corpus": to}, device_id_type=MESH)

    def in_copy(src, dst, chan, dz, dy):
        frm = source(dz, dy)
        rows = pl.ds(pl.multiple_of(frm * SLOTS, 16), SLOTS)
        return pltpu.make_async_remote_copy(
            src_ref=src.at[rows, :], dst_ref=dst.at[rows, :],
            send_sem=aa_send.at[chan, dz * SIDE + dy], recv_sem=aa_recv.at[chan, dz * SIDE + dy],
            device_id={"corpus": frm}, device_id_type=MESH)

    def start_out(src, dst, chan, dz, dy):
        rows = pl.ds(pl.multiple_of(c * SLOTS, 16), SLOTS)
        off = dz * SIDE + dy

        @pl.when(off == 0)
        def _():
            pltpu.make_async_copy(src.at[rows, :], dst.at[rows, :], aa_recv.at[chan, 0]).start()

        @pl.when(off != 0)
        def _():
            out_copy(src, dst, chan, dz, dy).start()

    def wait_in(src, dst, chan, dz, dy):
        rows = pl.ds(pl.multiple_of(c * SLOTS, 16), SLOTS)
        off = dz * SIDE + dy

        @pl.when(off == 0)
        def _():
            pltpu.make_async_copy(src.at[rows, :], dst.at[rows, :], aa_recv.at[chan, 0]).wait()

        @pl.when(off != 0)
        def _():
            in_copy(src, dst, chan, dz, dy).wait_recv()

    @pl.loop(0, 16)
    def _(i):
        n = 15 - i
        dz, dy = lax.div(n, SIDE), lax.rem(n, SIDE)
        to = peer(dz, dy)
        rows = pl.ds(pl.multiple_of(to * SLOTS, 16), SLOTS)
        qs[rows, :] = dot(r[rows, :], q[...]).astype(BF)
        start_out(qs, qr, 0, dz, dy)

    offs = offs_ref[...]
    for g in range(4):
        inv[g, :, :] = jnp.full((128, LANES), -1, I32)

    @pl.loop(0, 32)
    def _(k):
        for g in range(4):
            at = jnp.full((128, LANES), g * 32, I32) + k
            here = lane_pick(offs, at)
            inv[g, :, :] = jnp.where(here == lane, at, inv[g, :, :])

    @pl.loop(0, 8)
    def _(n):
        cols = pl.ds(pl.multiple_of(n * 256, 256), 256)
        xt[cols, :] = xcat[:, cols].T

    load_p.wait()

    sub = lax.broadcasted_iota(I32, (192, LANES), 0) & 7

    @pl.loop(0, 4)
    def _(k):
        dz = k ^ (k >> 1)
        zs = lax.rem(z + SIDE - dz, SIDE)

        @pl.loop(0, 4)
        def _(dy):
            wait_in(qs, qr, 0, dz, dy)

        rows = pl.ds(pl.multiple_of(zs * 192, 16), 192)
        acc = jnp.zeros((192, LANES), F32)
        for j in range(4):
            both = dot(qr[rows, :], p[j * 256:(j + 1) * 256, :], ((1,), (1,)))
            acc = jnp.where(sub == 2 * j, both[:, :128], acc)
            acc = jnp.where(sub == 2 * j + 1, both[:, 128:], acc)
        ss[rows, :] = acc

        @pl.loop(0, 4)
        def _(dy):
            start_out(ss, sr, 1, lax.rem(SIDE - dz, SIDE), lax.rem(SIDE - dy, SIDE))

    @pl.loop(0, 16)
    def _(i):
        wait_in(ss, sr, 1, lax.div(i, SIDE), lax.rem(i, SIDE))

    back = sr[...]
    s3[:, 0:128] = back.astype(BF)
    back = back - s3[:, 0:128].astype(F32)
    s3[:, 128:256] = back.astype(BF)
    back = back - s3[:, 128:256].astype(F32)
    s3[:, 256:384] = back.astype(BF)
    mine = jnp.zeros((128, LANES), F32)
    for g in range(4):
        three = dot(pmt[g, :, :], s3[...])
        dense = three[:, 0:128] + (three[:, 128:256] + three[:, 256:384])
        mine = jnp.where((lane >> 5) == g, lane_pick(dense, offs), mine)
    st[t, :, :] = mine

    def te_copy(i):
        return pltpu.make_async_remote_copy(
            src_ref=st.at[t], dst_ref=st.at[t],
            send_sem=te_send.at[i], recv_sem=te_recv.at[i],
            device_id={"tensor": lax.rem(t + i, 4)}, device_id_type=MESH)

    def te_in(i):
        frm = lax.rem(t + 4 - i, 4)
        return pltpu.make_async_remote_copy(
            src_ref=st.at[frm], dst_ref=st.at[frm],
            send_sem=te_send.at[i], recv_sem=te_recv.at[i],
            device_id={"tensor": frm}, device_id_type=MESH)

    for i in (2, 1, 3):
        te_copy(i).start()
    teacher = teacher_ref[...]
    teacher_top = jnp.max(teacher, axis=1, keepdims=True)
    teacher_lse = teacher_top + jnp.log(
        jnp.sum(jnp.exp(teacher - teacher_top), axis=1, keepdims=True))
    log_teacher = teacher - teacher_lse
    prob_teacher = jnp.exp(log_teacher)
    for i in (1, 3, 2):
        te_in(i).wait_recv()
    student = 50.0 * (((st[0, :, :] + st[1, :, :]) + st[2, :, :]) + st[3, :, :])
    top = jnp.max(student, axis=1, keepdims=True)
    log_student = student - (top + jnp.log(
        jnp.sum(jnp.exp(student - top), axis=1, keepdims=True)))
    dscore = (50.0 * (jnp.exp(log_student) - prob_teacher)).astype(BF).astype(F32)
    spread = jnp.zeros((ALL, LANES), F32)
    for g in range(4):
        at = inv[g, :, :]
        dense = jnp.where(at >= 0, lane_pick(dscore, jnp.maximum(at, 0)), 0.0)
        spread = spread + dot(pm[:, g * 128:(g + 1) * 128], dense.astype(BF))
    ds[...] = spread.astype(BF)

    @pl.loop(0, 16)
    def _(i):
        n = 15 - i
        start_out(ds, dr, 2, lax.div(n, SIDE), lax.rem(n, SIDE))

    terms = prob_teacher * (log_teacher - log_student)
    kl_ref[...] = jnp.sum(terms.T, axis=0, keepdims=True)

    @pl.loop(0, 4)
    def _(k):
        dz = k ^ (k >> 1)
        zs = lax.rem(z + SIDE - dz, SIDE)

        @pl.loop(0, 4)
        def _(dy):
            wait_in(ds, dr, 2, dz, dy)

        rows = pl.ds(pl.multiple_of(zs * 192, 16), 192)
        given = dr[rows, :].astype(F32)
        for j in range(8):
            dexp[:, j * 128:(j + 1) * 128] = jnp.where(sub == j, given, 0.0).astype(BF)

        @pl.loop(0, 4)
        def _(n):
            cols = pl.ds(pl.multiple_of(n * 256, 256), 256)
            ps[rows, cols] = dot(dexp[...], p[:, cols]).astype(BF)

        @pl.loop(0, 4)
        def _(dy):
            start_out(ps, pr, 3, lax.rem(SIDE - dz, SIDE), lax.rem(SIDE - dy, SIDE))

    @pl.loop(0, 16)
    def _(i):
        wait_in(ps, pr, 3, lax.div(i, SIDE), lax.rem(i, SIDE))

    @pl.loop(0, 4)
    def _(n):
        cols = pl.ds(pl.multiple_of(n * 256, 256), 256)
        qg2[0:128, cols] = dot(rt[...], pr[:, cols]).astype(BF)

    swap_qg = pltpu.make_async_remote_copy(
        src_ref=qg2.at[pl.ds(0, 128), :], dst_ref=qg2.at[pl.ds(128, 128), :],
        send_sem=fs_send.at[2], recv_sem=fs_recv.at[2],
        device_id={"fsdp": 1 - f}, device_id_type=MESH)
    swap_qg.start()
    swap_qg.wait_recv()

    first = (z, y)
    second = (y, z)

    def ring(half, stage):
        along_z = (half == 0) == (stage == 0)
        here = z if along_z else y

        def at(i):
            there = lax.rem(here + i, SIDE)
            dev = there * SIDE + y if along_z else z * SIDE + there
            return there, dev
        return here, at

    def send_piece(half, stage, i, src, dst, sem):
        _, at = ring(half, stage)
        _, dev = at(i)
        return pltpu.make_async_remote_copy(
            src_ref=src, dst_ref=dst,
            send_sem=ar_send.at[sem, half, i - 1], recv_sem=ar_recv.at[sem, half, i - 1],
            device_id={"corpus": dev}, device_id_type=MESH)

    for i in (2, 1, 3, 0):
        for half in range(2):
            here, at = ring(half, 0)
            there, _ = at(i)
            lhs = pl.ds(pl.multiple_of(half * 1024 + there * 256, 256), 256)

            @pl.loop(0, 4)
            def _(n, half=half, there=there, lhs=lhs, i=i):
                cols = pl.ds(pl.multiple_of(n * 256, 256), 256)
                prod = dot(xt[lhs, :], qg2[:, cols])
                if i == 0:
                    gown[half, :, cols] = prod
                else:
                    gsend[half, there, :, cols] = prod.astype(BF)

            if i != 0:
                send_piece(half, 0, i, gsend.at[half, there], grecv.at[half, here], 0).start()

    def frm(half, stage, i):
        here, _ = ring(half, stage)
        return lax.rem(here + SIDE - i, SIDE)

    def wait_piece(half, stage, i, dst, sem):
        send_piece(half, stage, i, dst, dst, sem).wait_recv()

    for half in range(2):
        for i in (1, 3, 2):
            wait_piece(half, 0, i, grecv.at[half, frm(half, 0, i)], 0)
        here0, _ = ring(half, 0)
        here1, at1 = ring(half, 1)
        for i in (2, 1, 3, 0):
            there, _ = at1(i)
            rows = pl.ds(pl.multiple_of(there * 64, 64), 64)
            total = gown[half, rows, :]
            for k in (1, 2, 3):
                total = total + grecv[half, frm(half, 0, k), rows, :].astype(F32)
            if i == 0:
                gown[half, rows, :] = total
            else:
                hsend[half, there, :, :] = total.astype(BF)
                send_piece(half, 1, i, hsend.at[half, there], hrecv.at[half, here1], 1).start()

    def out_rows(half, a, b):
        return pl.ds(pl.multiple_of(half * 1024 + a * 256 + b * 64, 64), 64)

    def out_quarter(half, a):
        return pl.ds(pl.multiple_of(half * 1024 + a * 256, 256), 256)

    for half in range(2):
        for i in (1, 3, 2):
            wait_piece(half, 1, i, hrecv.at[half, frm(half, 1, i)], 1)
        here0, _ = ring(half, 0)
        here1, _ = ring(half, 1)
        total = gown[half, pl.ds(pl.multiple_of(here1 * 64, 64), 64), :]
        for k in (1, 2, 3):
            total = total + hrecv[half, frm(half, 1, k), :, :].astype(F32)
        mine_rows = out_rows(half, here0, here1)
        hg_ref[mine_rows, :] = total.astype(BF)
        for i in (2, 1, 3):
            send_piece(half, 1, i, hg_ref.at[mine_rows, :], hg_ref.at[mine_rows, :], 2).start()

    for half in range(2):
        here0, _ = ring(half, 0)
        for i in (1, 3, 2):
            wait_piece(half, 1, i, hg_ref.at[out_rows(half, here0, frm(half, 1, i)), :], 2)
        quarter = out_quarter(half, here0)
        for i in (2, 1, 3):
            send_piece(half, 0, i, hg_ref.at[quarter, :], hg_ref.at[quarter, :], 3).start()

    for half in range(2):
        for i in (1, 3, 2):
            wait_piece(half, 0, i, hg_ref.at[out_quarter(half, frm(half, 0, i)), :], 3)

    swap_x.wait_send()
    swap_part.wait_send()
    swap_qg.wait_send()
    for i in (1, 2, 3):
        te_copy(i).wait_send()
    for chan, (src, dst) in enumerate(((qs, qr), (ss, sr), (ds, dr), (ps, pr))):
        @pl.loop(1, 16)
        def _(n, chan=chan, src=src, dst=dst):
            out_copy(src, dst, chan, lax.div(n, SIDE), lax.rem(n, SIDE)).wait_send()
    for half in range(2):
        here0, at0 = ring(half, 0)
        here1, at1 = ring(half, 1)
        mine_rows = out_rows(half, here0, here1)
        quarter = out_quarter(half, here0)
        for i in (1, 2, 3):
            send_piece(half, 0, i, gsend.at[half, at0(i)[0]], grecv.at[half, here0], 0).wait_send()
            send_piece(half, 1, i, hsend.at[half, at1(i)[0]], hrecv.at[half, here1], 1).wait_send()
            send_piece(half, 1, i, hg_ref.at[mine_rows, :], hg_ref.at[mine_rows, :], 2).wait_send()
            send_piece(half, 0, i, hg_ref.at[quarter, :], hg_ref.at[quarter, :], 3).wait_send()


def on_device(queries_in, head_weight, passages, teacher, cand_block, cand_offset, block_slot):
    vmem = pl.BlockSpec(memory_space=pltpu.VMEM)
    anywhere = pl.BlockSpec(memory_space=pl.ANY)
    V = pltpu.VMEM
    dma = pltpu.SemaphoreType.DMA
    kl, hg = pl.pallas_call(
        step_kernel,
        out_shape=(jax.ShapeDtypeStruct((1, 128), F32), jax.ShapeDtypeStruct((2048, 1024), BF)),
        in_specs=[anywhere, anywhere, anywhere, vmem, vmem, vmem, vmem],
        out_specs=(vmem, vmem),
        scratch_shapes=[
            V((256, 2048), BF), V((2048, 256), BF), V((2048, 1024), BF), V((1024, 1024), BF),
            V((128, 1024), F32), V((128, 1024), F32), V((128, 1024), F32), V((128, 1024), BF),
            V((4, 128, ALL), BF), V((ALL, 512), BF), V((ALL, 128), BF), V((128, ALL), BF),
            V((4, 128, LANES), I32),
            V((ALL, 1024), BF), V((ALL, 1024), BF), V((ALL, LANES), F32), V((ALL, LANES), F32),
            V((ALL, 384), BF), V((4, 128, LANES), F32), V((ALL, LANES), BF), V((ALL, LANES), BF),
            V((192, 1024), BF), V((ALL, 1024), BF), V((ALL, 1024), BF), V((256, 1024), BF),
            V((2, 4, 256, 1024), BF), V((2, 4, 256, 1024), BF), V((2, 256, 1024), F32),
            V((2, 4, 64, 1024), BF), V((2, 4, 64, 1024), BF),
            dma((3,)), dma((3,)), dma((3,)), dma((4, 16)), dma((4, 16)), dma((4,)), dma((4,)),
            dma((4, 2, 3)), dma((4, 2, 3)),
        ],
        compiler_params=pltpu.CompilerParams(
            collective_id=0, has_side_effects=True, vmem_limit_bytes=56 * 1024 * 1024),
    )(queries_in, head_weight, passages, teacher.reshape(128, 128), cand_offset.reshape(128, 128),
      cand_block, block_slot.reshape(1, 128))
    return kl.reshape(128), hg.astype(F32)


def solution(mesh):
    placed = (
        P(("corpus", "fsdp"), None),
        P("fsdp", "tensor"),
        P("corpus", "tensor"),
        P(("corpus", "fsdp"), None, None),
        P(("corpus", "fsdp"), None),
        P(("corpus", "fsdp"), None, None),
        P(),
    )
    return jax.shard_map(
        on_device,
        mesh=mesh,
        in_specs=placed,
        out_specs=(P(("corpus", "fsdp")), P("fsdp", "tensor")),
        check_vma=False,
    )
```

```python
import jax
import jax.numpy as jnp
from jax import lax
from jax.experimental import pallas as pl
from jax.experimental.pallas import tpu as pltpu
from jax.sharding import PartitionSpec as P

BF = jnp.bfloat16
F32 = jnp.float32
I32 = jnp.int32
SIDE = 4
SLOTS = 48
ALL = 768
LANES = 128
HALF = 512
MESH = pl.DeviceIdType.MESH
FAR = ((2, 2), (1, 2), (2, 1), (3, 2), (2, 3), (1, 1), (3, 3), (1, 3), (3, 1),
       (2, 0), (0, 2), (1, 0), (0, 1), (3, 0), (0, 3), (0, 0))


def dot(a, b, dims=((1,), (0,))):
    return lax.dot_general(a, b, (dims, ((), ())), preferred_element_type=F32)


def lane_pick(values, index):
    return jnp.take_along_axis(values, index, axis=1)


def step_kernel(x_hbm, w_hbm, p_hbm, teacher_ref, offs_ref, cand_ref, bslot_ref,
                kl_ref, hg_ref,
                xcat, xz, xzt, w, p, part_own, part_send, part_recv, q,
                pm, pmt, r, rtz, inv, offs_s,
                qs, qr, ss, sr, s3, dn, st, ds, dr, dexp, ps, pr, qga, qg2, qz,
                gown, hsend, hrecv,
                loc_sem, fs_send, fs_recv, aa_send, aa_recv, te_send, te_recv,
                xb_send, xb_recv, ql_send, ql_recv, qc_send, qc_recv,
                h_send, h_recv, s_send, s_recv, f_send, f_recv):
    c = lax.axis_index("corpus")
    f = lax.axis_index("fsdp")
    t = lax.axis_index("tensor")
    z = lax.div(c, SIDE)
    y = lax.rem(c, SIDE)
    sent = []
    looped = []

    def peer(dz, dy):
        return lax.rem(z + dz, SIDE) * SIDE + lax.rem(y + dy, SIDE)

    def source(dz, dy):
        return lax.rem(z + SIDE - dz, SIDE) * SIDE + lax.rem(y + SIDE - dy, SIDE)

    def half_cols(h):
        return pl.ds(h * HALF, HALF)

    own_cols = pl.ds(pl.multiple_of(f * 2048, 2048), 2048)
    other_cols = pl.ds(pl.multiple_of((1 - f) * 2048, 2048), 2048)
    load_x = pltpu.make_async_copy(
        x_hbm.at[:, own_cols], xcat.at[pl.ds(0, 128), :], loc_sem.at[0])
    load_w = pltpu.make_async_copy(w_hbm, w, loc_sem.at[1])
    load_p = pltpu.make_async_copy(p_hbm, p, loc_sem.at[2])
    load_x.start()
    load_w.start()
    load_p.start()

    barrier = pltpu.get_barrier_semaphore()
    pl.semaphore_signal(barrier, inc=1, device_id={"fsdp": 1 - f}, device_id_type=MESH)

    @pl.loop(1, 4)
    def _(i):
        pl.semaphore_signal(
            barrier, inc=1, device_id={"tensor": lax.rem(t + i, 4)}, device_id_type=MESH)

    @pl.loop(1, 16)
    def _(i):
        pl.semaphore_signal(
            barrier, inc=1, device_id={"corpus": peer(lax.div(i, SIDE), lax.rem(i, SIDE))},
            device_id_type=MESH)

    lane = lax.broadcasted_iota(I32, (128, LANES), 1)
    row = lax.broadcasted_iota(I32, (128, LANES), 0)
    slot_of = jnp.broadcast_to(bslot_ref[...].astype(F32), (128, LANES)).T
    hits = jnp.zeros((128, LANES), F32)
    slots = []
    for g in range(4):
        named = cand_ref[g:g + 1, :] == row
        slot = jnp.sum(jnp.where(named, slot_of, 0.0), axis=0, keepdims=True).astype(I32)
        slots.append(slot)
        hits = hits + jnp.where(slot == row, 1.0, 0.0)
    earlier = jnp.where(row < lane, 1.0, 0.0).astype(BF)
    before = dot(hits.astype(BF), earlier)
    places = []
    for g in range(4):
        rank = jnp.sum(jnp.where(slots[g] == row, before, 0.0), axis=0, keepdims=True).astype(I32)
        places.append((slots[g] >> 3) * SLOTS + rank * 8 + (slots[g] & 7))
    for n in range(4):
        place_row = lax.broadcasted_iota(I32, (192, LANES), 0) + n * 192
        total = jnp.zeros((192, LANES), F32)
        for g in range(4):
            one = jnp.where(places[g] == place_row, 1.0, 0.0)
            total = total + one
            pm[n * 192:(n + 1) * 192, g * 128:(g + 1) * 128] = one.astype(BF)
        r[n * 192:(n + 1) * 192, :] = total.astype(BF)

    pl.semaphore_wait(barrier, 19)

    def fs_copy(src, dst, k):
        return pltpu.make_async_remote_copy(
            src_ref=src, dst_ref=dst, send_sem=fs_send.at[k], recv_sem=fs_recv.at[k],
            device_id={"fsdp": 1 - f}, device_id_type=MESH)

    def begin(copy):
        copy.start()
        sent.append(copy)
        return copy

    swap_x = begin(fs_copy(x_hbm.at[:, other_cols], xcat.at[pl.ds(128, 128), :], 0))

    def view(ref, at, h):
        rows = pl.ds(pl.multiple_of(at * SLOTS, 16), SLOTS)
        return ref.at[rows, :] if h is None else ref.at[rows, half_cols(h)]

    def out_copy(src, dst, chan, h, dz, dy):
        to, k, n = peer(dz, dy), 0 if h is None else h, dz * SIDE + dy
        return pltpu.make_async_remote_copy(
            src_ref=view(src, to, h), dst_ref=view(dst, c, h),
            send_sem=aa_send.at[chan, k, n], recv_sem=aa_recv.at[chan, k, n],
            device_id={"corpus": to}, device_id_type=MESH)

    def in_copy(src, dst, chan, h, dz, dy):
        frm, k, n = source(dz, dy), 0 if h is None else h, dz * SIDE + dy
        return pltpu.make_async_remote_copy(
            src_ref=view(src, frm, h), dst_ref=view(dst, frm, h),
            send_sem=aa_send.at[chan, k, n], recv_sem=aa_recv.at[chan, k, n],
            device_id={"corpus": frm}, device_id_type=MESH)

    def self_copy(src, dst, chan, h):
        return pltpu.make_async_copy(
            view(src, c, h), view(dst, c, h), aa_recv.at[chan, 0 if h is None else h, 0])

    def start_out(src, dst, chan, h, dz, dy):
        off = dz * SIDE + dy

        @pl.when(off == 0)
        def _():
            self_copy(src, dst, chan, h).start()

        @pl.when(off != 0)
        def _():
            out_copy(src, dst, chan, h, dz, dy).start()

    def wait_in(src, dst, chan, h, dz, dy):
        off = dz * SIDE + dy

        @pl.when(off == 0)
        def _():
            self_copy(src, dst, chan, h).wait()

        @pl.when(off != 0)
        def _():
            in_copy(src, dst, chan, h, dz, dy).wait_recv()

    def order(k):
        return (3 - k) ^ ((3 - k) >> 1)

    def wait_group(src, dst, chan, h, dz):
        @pl.loop(0, 4)
        def _(k):
            wait_in(src, dst, chan, h, dz, order(k))

    def group_rows(dz):
        zs = lax.rem(z + SIDE - dz, SIDE)
        return zs, pl.ds(pl.multiple_of(zs * 192, 16), 192)

    def answer_group(src, dst, chan, h, dz):
        @pl.loop(0, 4)
        def _(k):
            start_out(src, dst, chan, h, lax.rem(SIDE - dz, SIDE),
                      lax.rem(SIDE - order(k), SIDE))

    def finish():
        for copy in sent:
            copy.wait_send()
        for src, dst, chan, h in looped:
            @pl.loop(1, 16)
            def _(n, src=src, dst=dst, chan=chan, h=h):
                out_copy(src, dst, chan, h, lax.div(n, SIDE), lax.rem(n, SIDE)).wait_send()

    load_x.wait()
    load_w.wait()

    @pl.loop(0, 4)
    def _(n):
        cols = pl.ds(pl.multiple_of(n * 256, 256), 256)
        part_own[:, cols] = dot(xcat[0:128, :], w[:, cols])

    swap_x.wait_recv()
    swaps = []
    for h in range(2):
        @pl.loop(2 * h, 2 * h + 2)
        def _(n):
            cols = pl.ds(pl.multiple_of(n * 256, 256), 256)
            part_send[:, cols] = dot(xcat[128:256, :], w[:, cols])

        swaps.append(begin(fs_copy(
            part_send.at[:, half_cols(h)], part_recv.at[:, half_cols(h)], 1 + h)))

    def along(half, stage, i):
        if (half == 0) == (stage == 0):
            there = lax.rem(z + i, SIDE)
            return there, there * SIDE + y
        there = lax.rem(y + i, SIDE)
        return there, z * SIDE + there

    def remote(src, dst, send_sem, recv_sem, dev):
        return pltpu.make_async_remote_copy(
            src_ref=src, dst_ref=dst, send_sem=send_sem, recv_sem=recv_sem,
            device_id={"corpus": dev}, device_id_type=MESH)

    def xb_copy(half, i):
        there, dev = along(half, 0, i)
        cols = pl.ds(pl.multiple_of(half * 1024 + there * 256, 256), 256)
        return remote(xcat.at[:, cols], xz.at[half, i - 1],
                      xb_send.at[half, i - 1], xb_recv.at[half, i - 1], dev)

    for i in (2, 1, 3):
        for half in range(2):
            begin(xb_copy(half, i))

    for h in range(2):
        cols = half_cols(h)
        swaps[h].wait_recv()
        q[:, cols] = (part_own[:, cols] + part_recv[:, cols]).astype(BF)

        @pl.loop(0, 4)
        def _(n, cols=cols):
            rows = pl.ds(pl.multiple_of(n * 192, 16), 192)
            qs[rows, cols] = dot(r[rows, :], q[:, cols]).astype(BF)

        for dz, dy in FAR:
            if (dz, dy) == (0, 0):
                self_copy(qs, qr, 0, h).start()
            else:
                begin(out_copy(qs, qr, 0, h, dz, dy))

    offs = offs_ref[...].astype(F32).T.astype(I32)
    offs_s[...] = offs
    for g in range(4):
        inv[g, :, :] = jnp.full((128, LANES), -1, I32)

    @pl.loop(0, 32)
    def _(k):
        for g in range(4):
            at = jnp.full((128, LANES), g * 32, I32) + k
            here = lane_pick(offs_s[...], at)
            inv[g, :, :] = jnp.where(here == lane, at, inv[g, :, :])

    for n in range(4):
        rows = slice(n * 192, (n + 1) * 192)
        rtz[n, :, :] = r[rows, :].astype(F32).T.astype(BF)
        for g in range(4):
            pmt[n, g * 128:(g + 1) * 128, :] = (
                pm[rows, g * 128:(g + 1) * 128].astype(F32).T.astype(BF))
    dn[...] = jnp.zeros((512, LANES), F32)
    qga[...] = jnp.zeros((128, 1024), F32)

    load_p.wait()
    sub = lax.broadcasted_iota(I32, (192, LANES), 0) & 7
    for h in range(2):
        @pl.loop(0, 4)
        def _(k, h=h):
            dz = order(k)
            zs, rows = group_rows(dz)
            wait_group(qs, qr, 0, h, dz)
            acc = jnp.zeros((192, LANES), F32)
            for j in range(4):
                both = dot(qr[rows, half_cols(h)], p[j * 256:(j + 1) * 256, half_cols(h)],
                           ((1,), (1,)))
                acc = jnp.where(sub == 2 * j, both[:, :128], acc)
                acc = jnp.where(sub == 2 * j + 1, both[:, 128:], acc)
            if h == 0:
                ss[rows, :] = acc
            else:
                ss[rows, :] = ss[rows, :] + acc
                answer_group(ss, sr, 1, None, dz)
    looped.append((ss, sr, 1, None))

    @pl.loop(0, 4)
    def _(k):
        dz = order(k)
        zs, rows = group_rows(dz)
        wait_group(ss, sr, 1, None, dz)
        back = sr[rows, :]
        s3[:, 0:128] = back.astype(BF)
        back = back - s3[:, 0:128].astype(F32)
        s3[:, 128:256] = back.astype(BF)
        back = back - s3[:, 128:256].astype(F32)
        s3[:, 256:384] = back.astype(BF)
        three = dot(pmt[zs, :, :], s3[...])
        dn[...] = dn[...] + (three[:, 0:128] + (three[:, 128:256] + three[:, 256:384]))

    mine = jnp.zeros((128, LANES), F32)
    for g in range(4):
        mine = jnp.where((lane >> 5) == g,
                         lane_pick(dn[g * 128:(g + 1) * 128, :], offs_s[...]), mine)
    st[t, :, :] = mine

    def te_copy(i):
        return pltpu.make_async_remote_copy(
            src_ref=st.at[t], dst_ref=st.at[t],
            send_sem=te_send.at[i], recv_sem=te_recv.at[i],
            device_id={"tensor": lax.rem(t + i, 4)}, device_id_type=MESH)

    def te_in(i):
        frm = lax.rem(t + 4 - i, 4)
        return pltpu.make_async_remote_copy(
            src_ref=st.at[frm], dst_ref=st.at[frm],
            send_sem=te_send.at[i], recv_sem=te_recv.at[i],
            device_id={"tensor": frm}, device_id_type=MESH)

    for i in (2, 1, 3):
        begin(te_copy(i))
    teacher = teacher_ref[...].T
    teacher_top = jnp.max(teacher, axis=1, keepdims=True)
    teacher_lse = teacher_top + jnp.log(
        jnp.sum(jnp.exp(teacher - teacher_top), axis=1, keepdims=True))
    log_teacher = teacher - teacher_lse
    prob_teacher = jnp.exp(log_teacher)
    for i in (1, 3, 2):
        te_in(i).wait_recv()
    student = 50.0 * (((st[0, :, :] + st[1, :, :]) + st[2, :, :]) + st[3, :, :])
    top = jnp.max(student, axis=1, keepdims=True)
    log_student = student - (top + jnp.log(
        jnp.sum(jnp.exp(student - top), axis=1, keepdims=True)))
    dscore = (50.0 * (jnp.exp(log_student) - prob_teacher)).astype(BF).astype(F32)
    for g in range(4):
        at = inv[g, :, :]
        dense = jnp.where(at >= 0, lane_pick(dscore, jnp.maximum(at, 0)), 0.0)
        dexp[g * 128:(g + 1) * 128, 0:128] = dense.astype(BF)

    @pl.loop(0, 4)
    def _(k):
        dz = lax.rem(SIDE - order(k), SIDE)
        zs, rows = group_rows(dz)
        ds[rows, :] = dot(pm[rows, :], dexp[0:512, 0:128]).astype(BF)
        answer_group(ds, dr, 2, None, dz)
    looped.append((ds, dr, 2, None))

    terms = prob_teacher * (log_teacher - log_student)
    kl_ref[...] = jnp.sum(terms.T, axis=0, keepdims=True)

    for h in range(2):
        @pl.loop(0, 4)
        def _(k, h=h):
            dz = order(k)
            zs, rows = group_rows(dz)
            if h == 0:
                wait_group(ds, dr, 2, None, dz)
                given = dr[rows, :].astype(F32)
                for j in range(8):
                    dexp[rows, j * 128:(j + 1) * 128] = jnp.where(sub == j, given, 0.0).astype(BF)

            @pl.loop(2 * h, 2 * h + 2)
            def _(n):
                cols = pl.ds(pl.multiple_of(n * 256, 256), 256)
                ps[rows, cols] = dot(dexp[rows, :], p[:, cols]).astype(BF)

            answer_group(ps, pr, 3, h, dz)
        looped.append((ps, pr, 3, h))

    def wait_recv(dst, send_sem, recv_sem):
        remote(dst, dst, send_sem, recv_sem, lax.rem(c + 1, 16)).wait_recv()

    for half in range(2):
        here, _ = along(half, 0, 0)
        cols = pl.ds(pl.multiple_of(half * 1024 + here * 256, 256), 256)
        xzt[half, 0, :, :] = xcat[:, cols].T
        for i in (1, 3, 2):
            wait_recv(xz.at[half, i - 1], xb_send.at[half, i - 1], xb_recv.at[half, i - 1])
            xzt[half, i, :, :] = xz[half, i - 1, :, :].T

    def ql_copy(src, axis, h, i, slot):
        _, dev = along(axis, 0, i)
        return remote(src, qz.at[axis, slot - 1, pl.ds(0, 128), half_cols(h)],
                      ql_send.at[axis, h, slot - 1], ql_recv.at[axis, h, slot - 1], dev)

    def ql_wait(axis, h, slot):
        wait_recv(qz.at[axis, slot - 1, pl.ds(0, 128), half_cols(h)],
                  ql_send.at[axis, h, slot - 1], ql_recv.at[axis, h, slot - 1])

    def qc_copy(axis, h, slot):
        return pltpu.make_async_remote_copy(
            src_ref=qz.at[axis, slot - 1, pl.ds(0, 128), half_cols(h)],
            dst_ref=qz.at[axis, slot - 1, pl.ds(128, 128), half_cols(h)],
            send_sem=qc_send.at[axis, h, slot - 1], recv_sem=qc_recv.at[axis, h, slot - 1],
            device_id={"fsdp": 1 - f}, device_id_type=MESH)

    swap_q = []
    for h in range(2):
        cols = half_cols(h)

        @pl.loop(0, 4)
        def _(k, h=h, cols=cols):
            dz = order(k)
            zs, rows = group_rows(dz)
            wait_group(ps, pr, 3, h, dz)
            qga[:, cols] = qga[:, cols] + dot(rtz[zs, :, :], pr[rows, cols])

        qg2[0:128, cols] = qga[:, cols].astype(BF)
        mine = qg2.at[pl.ds(0, 128), cols]
        for i, slot in ((1, 1), (3, 3)):
            for axis in range(2):
                begin(ql_copy(mine, axis, h, i, slot))
        swap_q.append(begin(fs_copy(mine, qg2.at[pl.ds(128, 128), cols], 3 + h)))

    for h in range(2):
        on = 1 if h == 0 else 3
        for slot in (on, 4 - on):
            for axis in range(2):
                ql_wait(axis, h, slot)
                if slot == on:
                    begin(ql_copy(qz.at[axis, slot - 1, pl.ds(0, 128), half_cols(h)],
                                  axis, h, on, 2))
                begin(qc_copy(axis, h, slot))

    for h in range(2):
        cols = half_cols(h)
        swap_q[h].wait_recv()
        for half in range(2):
            gown[half, :, cols] = dot(xzt[half, 0, :, :], qg2[:, cols])
        for slot in (1, 3):
            for half in range(2):
                qc_copy(half, h, slot).wait_recv()
                gown[half, :, cols] = gown[half, :, cols] + dot(
                    xzt[half, slot, :, :], qz[half, slot - 1, :, cols])
        for half in range(2):
            ql_wait(half, h, 2)
            begin(qc_copy(half, h, 2))
        for half in range(2):
            qc_copy(half, h, 2).wait_recv()
            gown[half, :, cols] = gown[half, :, cols] + dot(
                xzt[half, 2, :, :], qz[half, 1, :, cols])
            for i in (2, 1, 3):
                there, dev = along(half, 1, i)
                rows = pl.ds(pl.multiple_of(there * 64, 64), 64)
                hsend[half, i - 1, :, cols] = gown[half, rows, cols].astype(BF)
                begin(remote(hsend.at[half, i - 1, :, cols], hrecv.at[half, i - 1, :, cols],
                             h_send.at[half, h, i - 1], h_recv.at[half, h, i - 1], dev))

    def piece(half, h, i, j):
        a, _ = along(half, 0, SIDE - i)
        b, _ = along(half, 1, SIDE - j)
        rows = pl.ds(pl.multiple_of(half * 1024 + a * 256 + b * 64, 64), 64)
        return hg_ref.at[rows, half_cols(h)]

    def second(half, h, j, i, slot):
        ref = piece(half, h, 0, j)
        _, dev = along(half, 1, i)
        begin(remote(ref, ref, s_send.at[half, h, slot - 1], s_recv.at[half, h, slot - 1], dev))

    def second_wait(half, h, slot):
        wait_recv(piece(half, h, 0, slot), s_send.at[half, h, slot - 1],
                  s_recv.at[half, h, slot - 1])

    def first(half, h, j, k, i, slot):
        ref = piece(half, h, k, j)
        _, dev = along(half, 0, i)
        begin(remote(ref, ref, f_send.at[half, h, j, slot - 1],
                     f_recv.at[half, h, j, slot - 1], dev))

    def first_wait(half, h, j, slot):
        wait_recv(piece(half, h, slot, j), f_send.at[half, h, j, slot - 1],
                  f_recv.at[half, h, j, slot - 1])

    both = [(h, half) for h in range(2) for half in range(2)]
    for h, half in both:
        cols = half_cols(h)
        for i in (1, 3, 2):
            wait_recv(hrecv.at[half, i - 1, :, cols], h_send.at[half, h, i - 1],
                      h_recv.at[half, h, i - 1])
        here, _ = along(half, 1, 0)
        total = gown[half, pl.ds(pl.multiple_of(here * 64, 64), 64), cols]
        for i in (1, 2, 3):
            total = total + hrecv[half, i - 1, :, cols].astype(F32)
        a, _ = along(half, 0, 0)
        hg_ref[pl.ds(pl.multiple_of(half * 1024 + a * 256 + here * 64, 64), 64), cols] = (
            total.astype(BF))
        for i in (1, 3):
            second(half, h, 0, i, i)
            first(half, h, 0, 0, i, i)

    for h, half in both:
        on = 1 if h == 0 else 3
        for slot in (on, 4 - on):
            second_wait(half, h, slot)
            if slot == on:
                second(half, h, slot, on, 2)
            for i in (1, 3):
                first(half, h, slot, 0, i, i)

    def pass_on(h, half, j):
        on = 1 if h == 0 else 3
        first_wait(half, h, j, on)
        first(half, h, j, on, on, 2)

    for h, half in both:
        pass_on(h, half, 0)
    for h, half in both:
        second_wait(half, h, 2)
        for i in (1, 3):
            first(half, h, 2, 0, i, i)
    for j in (1, 3, 2):
        for h, half in both:
            pass_on(h, half, j)
    for h, half in both:
        on = 1 if h == 0 else 3
        for j in (0, 1, 3, 2):
            first_wait(half, h, j, 4 - on)
            first_wait(half, h, j, 2)
    finish()


def on_device(queries_in, head_weight, passages, teacher, cand_block, cand_offset, block_slot):
    vmem = pl.BlockSpec(memory_space=pltpu.VMEM)
    anywhere = pl.BlockSpec(memory_space=pl.ANY)
    V = pltpu.VMEM
    dma = pltpu.SemaphoreType.DMA
    kl, hg = pl.pallas_call(
        step_kernel,
        out_shape=(jax.ShapeDtypeStruct((1, 128), F32), jax.ShapeDtypeStruct((2048, 1024), BF)),
        in_specs=[anywhere, anywhere, anywhere, vmem, vmem, vmem, vmem],
        out_specs=(vmem, vmem),
        scratch_shapes=[
            V((256, 2048), BF), V((2, 3, 256, 256), BF), V((2, 4, 256, 256), BF),
            V((2048, 1024), BF), V((1024, 1024), BF),
            V((128, 1024), F32), V((128, 1024), F32), V((128, 1024), F32), V((128, 1024), BF),
            V((ALL, 512), BF), V((4, 512, 192), BF), V((ALL, 128), BF), V((4, 128, 192), BF),
            V((4, 128, LANES), I32), V((128, LANES), I32),
            V((ALL, 1024), BF), V((ALL, 1024), BF), V((ALL, LANES), F32), V((ALL, LANES), F32),
            V((192, 384), BF), V((512, LANES), F32), V((4, 128, LANES), F32),
            V((ALL, LANES), BF), V((ALL, LANES), BF),
            V((ALL, 1024), BF), V((ALL, 1024), BF), V((ALL, 1024), BF),
            V((128, 1024), F32), V((256, 1024), BF), V((2, 3, 256, 1024), BF),
            V((2, 256, 1024), F32), V((2, 3, 64, 1024), BF), V((2, 3, 64, 1024), BF),
            dma((3,)), dma((5,)), dma((5,)), dma((4, 2, 16)), dma((4, 2, 16)),
            dma((4,)), dma((4,)),
            dma((2, 3)), dma((2, 3)), dma((2, 2, 3)), dma((2, 2, 3)), dma((2, 2, 3)),
            dma((2, 2, 3)), dma((2, 2, 3)), dma((2, 2, 3)), dma((2, 2, 3)), dma((2, 2, 3)),
            dma((2, 2, 4, 3)), dma((2, 2, 4, 3)),
        ],
        compiler_params=pltpu.CompilerParams(
            collective_id=0, has_side_effects=True, vmem_limit_bytes=56 * 1024 * 1024),
    )(queries_in, head_weight, passages, teacher.reshape(128, 128).T,
      cand_offset.reshape(128, 128).T, cand_block.T, block_slot.reshape(1, 128))
    return kl.reshape(128), hg.astype(F32)


def solution(mesh):
    placed = (
        P(("corpus", "fsdp"), None),
        P("fsdp", "tensor"),
        P("corpus", "tensor"),
        P(("corpus", "fsdp"), None, None),
        P(("corpus", "fsdp"), None),
        P(("corpus", "fsdp"), None, None),
        P(),
    )
    return jax.shard_map(
        on_device,
        mesh=mesh,
        in_specs=placed,
        out_specs=(P(("corpus", "fsdp")), P("fsdp", "tensor")),
        check_vma=False,
    )
```

```python
import jax
import jax.numpy as jnp
from jax import lax
from jax.experimental import pallas as pl
from jax.experimental.pallas import tpu as pltpu
from jax.sharding import PartitionSpec as P

BF = jnp.bfloat16
F32 = jnp.float32
I32 = jnp.int32
SIDE = 4
SLOTS = 48
ALL = 768
LANES = 128
VLIM = 62_816_256
HALF = 512
MESH = pl.DeviceIdType.MESH
FAR = ((2, 2), (1, 2), (2, 1), (3, 2), (2, 3), (1, 1), (3, 3), (1, 3), (3, 1),
       (2, 0), (0, 2), (1, 0), (0, 1), (3, 0), (0, 3), (0, 0))


def dot(a, b, dims=((1,), (0,))):
    return lax.dot_general(a, b, (dims, ((), ())), preferred_element_type=F32)


def lane_pick(values, index):
    return jnp.take_along_axis(values, index, axis=1)


def step_kernel(x_hbm, w_hbm, p_hbm, teacher_ref, offs_ref, cand_ref, bslot_ref,
                kl_ref, hg_ref,
                xcat, xz, xzt, w, p, part_own, part_send, part_recv, q,
                pm, pmt, r, rtz, inv, offs_s,
                qs, qr, ss, sr, s3, dn, st, ds, dr, dexp, ps, pr, qga, qg2, qz,
                gown, hsend, hrecv,
                loc_sem, fs_send, fs_recv, aa_send, aa_recv, te_send, te_recv,
                xb_send, xb_recv, ql_send, ql_recv, qc_send, qc_recv,
                h_send, h_recv, s_send, s_recv, f_send, f_recv):
    c = lax.axis_index("corpus")
    f = lax.axis_index("fsdp")
    t = lax.axis_index("tensor")
    z = lax.div(c, SIDE)
    y = lax.rem(c, SIDE)
    sent = []
    looped = []

    def peer(dz, dy):
        return lax.rem(z + dz, SIDE) * SIDE + lax.rem(y + dy, SIDE)

    def source(dz, dy):
        return lax.rem(z + SIDE - dz, SIDE) * SIDE + lax.rem(y + SIDE - dy, SIDE)

    def half_cols(h):
        return pl.ds(h * HALF, HALF)

    own_cols = pl.ds(pl.multiple_of(f * 2048, 2048), 2048)
    other_cols = pl.ds(pl.multiple_of((1 - f) * 2048, 2048), 2048)
    load_x = pltpu.make_async_copy(
        x_hbm.at[:, own_cols], xcat.at[pl.ds(0, 128), :], loc_sem.at[0])
    load_w = pltpu.make_async_copy(w_hbm, w, loc_sem.at[1])
    load_p = pltpu.make_async_copy(p_hbm, p, loc_sem.at[2])
    load_x.start()
    load_w.start()
    load_p.start()

    barrier = pltpu.get_barrier_semaphore()
    pl.semaphore_signal(barrier, inc=1, device_id={"fsdp": 1 - f}, device_id_type=MESH)

    @pl.loop(1, 4)
    def _(i):
        pl.semaphore_signal(
            barrier, inc=1, device_id={"tensor": lax.rem(t + i, 4)}, device_id_type=MESH)

    @pl.loop(1, 16)
    def _(i):
        pl.semaphore_signal(
            barrier, inc=1, device_id={"corpus": peer(lax.div(i, SIDE), lax.rem(i, SIDE))},
            device_id_type=MESH)

    lane = lax.broadcasted_iota(I32, (128, LANES), 1)
    row = lax.broadcasted_iota(I32, (128, LANES), 0)
    slot_of = jnp.broadcast_to(bslot_ref[...].astype(F32), (128, LANES)).T
    hits = jnp.zeros((128, LANES), F32)
    slots = []
    for g in range(4):
        named = cand_ref[g:g + 1, :] == row
        slot = jnp.sum(jnp.where(named, slot_of, 0.0), axis=0, keepdims=True).astype(I32)
        slots.append(slot)
        hits = hits + jnp.where(slot == row, 1.0, 0.0)
    earlier = jnp.where(row < lane, 1.0, 0.0).astype(BF)
    before = dot(hits.astype(BF), earlier)
    places = []
    for g in range(4):
        rank = jnp.sum(jnp.where(slots[g] == row, before, 0.0), axis=0, keepdims=True).astype(I32)
        places.append((slots[g] >> 3) * SLOTS + rank * 8 + (slots[g] & 7))
    pl.semaphore_wait(barrier, 19)

    def fs_copy(src, dst, k):
        return pltpu.make_async_remote_copy(
            src_ref=src, dst_ref=dst, send_sem=fs_send.at[k], recv_sem=fs_recv.at[k],
            device_id={"fsdp": 1 - f}, device_id_type=MESH)

    def begin(copy):
        copy.start()
        sent.append(copy)
        return copy

    swap_x = begin(fs_copy(x_hbm.at[:, other_cols], xcat.at[pl.ds(128, 128), :], 0))

    for n in range(4):
        place_row = lax.broadcasted_iota(I32, (192, LANES), 0) + n * 192
        total = jnp.zeros((192, LANES), F32)
        for g in range(4):
            one = jnp.where(places[g] == place_row, 1.0, 0.0)
            total = total + one
            pm[n * 192:(n + 1) * 192, g * 128:(g + 1) * 128] = one.astype(BF)
        r[n * 192:(n + 1) * 192, :] = total.astype(BF)

    def view(ref, at, h):
        rows = pl.ds(pl.multiple_of(at * SLOTS, 16), SLOTS)
        return ref.at[rows, :] if h is None else ref.at[rows, half_cols(h)]

    def out_copy(src, dst, chan, h, dz, dy):
        to, k, n = peer(dz, dy), 0 if h is None else h, dz * SIDE + dy
        return pltpu.make_async_remote_copy(
            src_ref=view(src, to, h), dst_ref=view(dst, c, h),
            send_sem=aa_send.at[chan, k, n], recv_sem=aa_recv.at[chan, k, n],
            device_id={"corpus": to}, device_id_type=MESH)

    def in_copy(src, dst, chan, h, dz, dy):
        frm, k, n = source(dz, dy), 0 if h is None else h, dz * SIDE + dy
        return pltpu.make_async_remote_copy(
            src_ref=view(src, frm, h), dst_ref=view(dst, frm, h),
            send_sem=aa_send.at[chan, k, n], recv_sem=aa_recv.at[chan, k, n],
            device_id={"corpus": frm}, device_id_type=MESH)

    def self_copy(src, dst, chan, h):
        return pltpu.make_async_copy(
            view(src, c, h), view(dst, c, h), aa_recv.at[chan, 0 if h is None else h, 0])

    def start_out(src, dst, chan, h, dz, dy):
        off = dz * SIDE + dy

        @pl.when(off == 0)
        def _():
            self_copy(src, dst, chan, h).start()

        @pl.when(off != 0)
        def _():
            out_copy(src, dst, chan, h, dz, dy).start()

    def wait_in(src, dst, chan, h, dz, dy):
        off = dz * SIDE + dy

        @pl.when(off == 0)
        def _():
            self_copy(src, dst, chan, h).wait()

        @pl.when(off != 0)
        def _():
            in_copy(src, dst, chan, h, dz, dy).wait_recv()

    def order(k):
        return (3 - k) ^ ((3 - k) >> 1)

    def wait_group(src, dst, chan, h, dz):
        @pl.loop(0, 4)
        def _(k):
            wait_in(src, dst, chan, h, dz, order(k))

    def group_rows(dz):
        zs = lax.rem(z + SIDE - dz, SIDE)
        return zs, pl.ds(pl.multiple_of(zs * 192, 16), 192)

    def answer_group(src, dst, chan, h, dz):
        @pl.loop(0, 4)
        def _(k):
            start_out(src, dst, chan, h, lax.rem(SIDE - dz, SIDE),
                      lax.rem(SIDE - order(k), SIDE))

    def finish():
        for copy in sent:
            copy.wait_send()
        for src, dst, chan, h in looped:
            @pl.loop(1, 16)
            def _(n, src=src, dst=dst, chan=chan, h=h):
                out_copy(src, dst, chan, h, lax.div(n, SIDE), lax.rem(n, SIDE)).wait_send()

    def along(half, stage, i):
        if (half == 0) == (stage == 0):
            there = lax.rem(z + i, SIDE)
            return there, there * SIDE + y
        there = lax.rem(y + i, SIDE)
        return there, z * SIDE + there

    def remote(src, dst, send_sem, recv_sem, dev):
        return pltpu.make_async_remote_copy(
            src_ref=src, dst_ref=dst, send_sem=send_sem, recv_sem=recv_sem,
            device_id={"corpus": dev}, device_id_type=MESH)

    def xb_copy(half, i):
        there, dev = along(half, 0, i)
        cols = pl.ds(pl.multiple_of(half * 1024 + there * 256, 256), 256)
        return remote(xcat.at[:, cols], xz.at[half, i - 1],
                      xb_send.at[half, i - 1], xb_recv.at[half, i - 1], dev)

    load_x.wait()
    swap_x.wait_recv()
    for i in (2, 1, 3):
        for half in range(2):
            begin(xb_copy(half, i))

    load_w.wait()
    swaps = []
    for h in range(2):
        @pl.loop(2 * h, 2 * h + 2)
        def _(n):
            cols = pl.ds(pl.multiple_of(n * 256, 256), 256)
            rows = dot(xcat[...], w[:, cols])
            part_own[:, cols] = rows[0:128, :]
            part_send[:, cols] = rows[128:256, :]

        swaps.append(begin(fs_copy(
            part_send.at[:, half_cols(h)], part_recv.at[:, half_cols(h)], 1 + h)))

    for h in range(2):
        cols = half_cols(h)
        swaps[h].wait_recv()
        q[:, cols] = (part_own[:, cols] + part_recv[:, cols]).astype(BF)

        @pl.loop(0, 4)
        def _(n, cols=cols):
            rows = pl.ds(pl.multiple_of(n * 192, 16), 192)
            qs[rows, cols] = dot(r[rows, :], q[:, cols]).astype(BF)

        for dz, dy in FAR:
            if (dz, dy) == (0, 0):
                self_copy(qs, qr, 0, h).start()
            else:
                begin(out_copy(qs, qr, 0, h, dz, dy))

    offs = offs_ref[...].astype(F32).T.astype(I32)
    offs_s[...] = offs
    for g in range(4):
        inv[g, :, :] = jnp.full((128, LANES), -1, I32)

    @pl.loop(0, 32)
    def _(k):
        for g in range(4):
            at = jnp.full((128, LANES), g * 32, I32) + k
            here = lane_pick(offs_s[...], at)
            inv[g, :, :] = jnp.where(here == lane, at, inv[g, :, :])

    for n in range(4):
        rows = slice(n * 192, (n + 1) * 192)
        rtz[n, :, :] = r[rows, :].astype(F32).T.astype(BF)
        for g in range(4):
            pmt[n, g * 128:(g + 1) * 128, :] = (
                pm[rows, g * 128:(g + 1) * 128].astype(F32).T.astype(BF))
    dn[...] = jnp.zeros((512, LANES), F32)
    qga[...] = jnp.zeros((128, 1024), F32)

    load_p.wait()
    sub = lax.broadcasted_iota(I32, (192, LANES), 0) & 7
    for h in range(2):
        @pl.loop(0, 4)
        def _(k, h=h):
            dz = order(k)
            zs, rows = group_rows(dz)
            wait_group(qs, qr, 0, h, dz)
            acc = jnp.zeros((192, LANES), F32)
            for j in range(4):
                both = dot(qr[rows, half_cols(h)], p[j * 256:(j + 1) * 256, half_cols(h)],
                           ((1,), (1,)))
                acc = jnp.where(sub == 2 * j, both[:, :128], acc)
                acc = jnp.where(sub == 2 * j + 1, both[:, 128:], acc)
            if h == 0:
                ss[rows, :] = acc
            else:
                ss[rows, :] = ss[rows, :] + acc
                answer_group(ss, sr, 1, None, dz)
    looped.append((ss, sr, 1, None))

    @pl.loop(0, 4)
    def _(k):
        dz = order(k)
        zs, rows = group_rows(dz)
        wait_group(ss, sr, 1, None, dz)
        back = sr[rows, :]
        s3[:, 0:128] = back.astype(BF)
        back = back - s3[:, 0:128].astype(F32)
        s3[:, 128:256] = back.astype(BF)
        back = back - s3[:, 128:256].astype(F32)
        s3[:, 256:384] = back.astype(BF)
        three = dot(pmt[zs, :, :], s3[...])
        dn[...] = dn[...] + (three[:, 0:128] + (three[:, 128:256] + three[:, 256:384]))

    mine = jnp.zeros((128, LANES), F32)
    for g in range(4):
        mine = jnp.where((lane >> 5) == g,
                         lane_pick(dn[g * 128:(g + 1) * 128, :], offs_s[...]), mine)
    st[t, :, :] = mine

    def te_copy(i):
        return pltpu.make_async_remote_copy(
            src_ref=st.at[t], dst_ref=st.at[t],
            send_sem=te_send.at[i], recv_sem=te_recv.at[i],
            device_id={"tensor": lax.rem(t + i, 4)}, device_id_type=MESH)

    def te_in(i):
        frm = lax.rem(t + 4 - i, 4)
        return pltpu.make_async_remote_copy(
            src_ref=st.at[frm], dst_ref=st.at[frm],
            send_sem=te_send.at[i], recv_sem=te_recv.at[i],
            device_id={"tensor": frm}, device_id_type=MESH)

    for i in (2, 1, 3):
        begin(te_copy(i))
    teacher = teacher_ref[...].T
    teacher_top = jnp.max(teacher, axis=1, keepdims=True)
    teacher_lse = teacher_top + jnp.log(
        jnp.sum(jnp.exp(teacher - teacher_top), axis=1, keepdims=True))
    log_teacher = teacher - teacher_lse
    prob_teacher = jnp.exp(log_teacher)
    for i in (1, 3, 2):
        te_in(i).wait_recv()
    student = 50.0 * (((st[0, :, :] + st[1, :, :]) + st[2, :, :]) + st[3, :, :])
    top = jnp.max(student, axis=1, keepdims=True)
    log_student = student - (top + jnp.log(
        jnp.sum(jnp.exp(student - top), axis=1, keepdims=True)))
    dscore = (50.0 * (jnp.exp(log_student) - prob_teacher)).astype(BF).astype(F32)
    for g in range(4):
        at = inv[g, :, :]
        dense = jnp.where(at >= 0, lane_pick(dscore, jnp.maximum(at, 0)), 0.0)
        dexp[g * 128:(g + 1) * 128, 0:128] = dense.astype(BF)

    @pl.loop(0, 4)
    def _(k):
        dz = lax.rem(SIDE - order(k), SIDE)
        zs, rows = group_rows(dz)
        ds[rows, :] = dot(pm[rows, :], dexp[0:512, 0:128]).astype(BF)
        answer_group(ds, dr, 2, None, dz)
    looped.append((ds, dr, 2, None))

    terms = prob_teacher * (log_teacher - log_student)
    kl_ref[...] = jnp.sum(terms.T, axis=0, keepdims=True)

    for h in range(2):
        @pl.loop(0, 4)
        def _(k, h=h):
            dz = order(k)
            zs, rows = group_rows(dz)
            if h == 0:
                wait_group(ds, dr, 2, None, dz)
                given = dr[rows, :].astype(F32)
                for j in range(8):
                    dexp[rows, j * 128:(j + 1) * 128] = jnp.where(sub == j, given, 0.0).astype(BF)

            @pl.loop(2 * h, 2 * h + 2)
            def _(n):
                cols = pl.ds(pl.multiple_of(n * 256, 256), 256)
                ps[rows, cols] = dot(dexp[rows, :], p[:, cols]).astype(BF)

            answer_group(ps, pr, 3, h, dz)
        looped.append((ps, pr, 3, h))

    def wait_recv(dst, send_sem, recv_sem):
        remote(dst, dst, send_sem, recv_sem, lax.rem(c + 1, 16)).wait_recv()

    for half in range(2):
        here, _ = along(half, 0, 0)
        cols = pl.ds(pl.multiple_of(half * 1024 + here * 256, 256), 256)
        xzt[half, 0, :, :] = xcat[:, cols].T
        for i in (1, 3, 2):
            wait_recv(xz.at[half, i - 1], xb_send.at[half, i - 1], xb_recv.at[half, i - 1])
            xzt[half, i, :, :] = xz[half, i - 1, :, :].T

    def ql_copy(src, axis, h, i, slot):
        _, dev = along(axis, 0, i)
        return remote(src, qz.at[axis, slot - 1, pl.ds(0, 128), half_cols(h)],
                      ql_send.at[axis, h, slot - 1], ql_recv.at[axis, h, slot - 1], dev)

    def ql_wait(axis, h, slot):
        wait_recv(qz.at[axis, slot - 1, pl.ds(0, 128), half_cols(h)],
                  ql_send.at[axis, h, slot - 1], ql_recv.at[axis, h, slot - 1])

    def qc_copy(axis, h, slot):
        return pltpu.make_async_remote_copy(
            src_ref=qz.at[axis, slot - 1, pl.ds(0, 128), half_cols(h)],
            dst_ref=qz.at[axis, slot - 1, pl.ds(128, 128), half_cols(h)],
            send_sem=qc_send.at[axis, h, slot - 1], recv_sem=qc_recv.at[axis, h, slot - 1],
            device_id={"fsdp": 1 - f}, device_id_type=MESH)

    swap_q = []
    for h in range(2):
        cols = half_cols(h)

        @pl.loop(0, 4)
        def _(k, h=h, cols=cols):
            dz = order(k)
            zs, rows = group_rows(dz)
            wait_group(ps, pr, 3, h, dz)
            qga[:, cols] = qga[:, cols] + dot(rtz[zs, :, :], pr[rows, cols])

        qg2[0:128, cols] = qga[:, cols].astype(BF)
        mine = qg2.at[pl.ds(0, 128), cols]
        for i, slot in ((1, 1), (3, 3)):
            for axis in range(2):
                begin(ql_copy(mine, axis, h, i, slot))
        swap_q.append(begin(fs_copy(mine, qg2.at[pl.ds(128, 128), cols], 3 + h)))

    for h in range(2):
        on = 1 if h == 0 else 3
        for slot in (on, 4 - on):
            for axis in range(2):
                ql_wait(axis, h, slot)
                if slot == on:
                    begin(ql_copy(qz.at[axis, slot - 1, pl.ds(0, 128), half_cols(h)],
                                  axis, h, on, 2))
                begin(qc_copy(axis, h, slot))

    for h in range(2):
        cols = half_cols(h)
        swap_q[h].wait_recv()
        for half in range(2):
            gown[half, :, cols] = dot(xzt[half, 0, :, :], qg2[:, cols])
        for slot in (1, 3):
            for half in range(2):
                qc_copy(half, h, slot).wait_recv()
                gown[half, :, cols] = gown[half, :, cols] + dot(
                    xzt[half, slot, :, :], qz[half, slot - 1, :, cols])
        for half in range(2):
            ql_wait(half, h, 2)
            begin(qc_copy(half, h, 2))
        for half in range(2):
            qc_copy(half, h, 2).wait_recv()
            gown[half, :, cols] = gown[half, :, cols] + dot(
                xzt[half, 2, :, :], qz[half, 1, :, cols])
            for i in (2, 1, 3):
                there, dev = along(half, 1, i)
                rows = pl.ds(pl.multiple_of(there * 64, 64), 64)
                hsend[half, i - 1, :, cols] = gown[half, rows, cols].astype(BF)
                begin(remote(hsend.at[half, i - 1, :, cols], hrecv.at[half, i - 1, :, cols],
                             h_send.at[half, h, i - 1], h_recv.at[half, h, i - 1], dev))

    def piece(half, h, i, j):
        a, _ = along(half, 0, SIDE - i)
        b, _ = along(half, 1, SIDE - j)
        rows = pl.ds(pl.multiple_of(half * 1024 + a * 256 + b * 64, 64), 64)
        return hg_ref.at[rows, half_cols(h)]

    def second(half, h, j, i, slot):
        ref = piece(half, h, 0, j)
        _, dev = along(half, 1, i)
        begin(remote(ref, ref, s_send.at[half, h, slot - 1], s_recv.at[half, h, slot - 1], dev))

    def second_wait(half, h, slot):
        wait_recv(piece(half, h, 0, slot), s_send.at[half, h, slot - 1],
                  s_recv.at[half, h, slot - 1])

    def first(half, h, j, k, i, slot):
        ref = piece(half, h, k, j)
        _, dev = along(half, 0, i)
        begin(remote(ref, ref, f_send.at[half, h, j, slot - 1],
                     f_recv.at[half, h, j, slot - 1], dev))

    def first_wait(half, h, j, slot):
        wait_recv(piece(half, h, slot, j), f_send.at[half, h, j, slot - 1],
                  f_recv.at[half, h, j, slot - 1])

    both = [(h, half) for h in range(2) for half in range(2)]
    for h, half in both:
        cols = half_cols(h)
        for i in (1, 3, 2):
            wait_recv(hrecv.at[half, i - 1, :, cols], h_send.at[half, h, i - 1],
                      h_recv.at[half, h, i - 1])
        here, _ = along(half, 1, 0)
        total = gown[half, pl.ds(pl.multiple_of(here * 64, 64), 64), cols]
        for i in (1, 2, 3):
            total = total + hrecv[half, i - 1, :, cols].astype(F32)
        a, _ = along(half, 0, 0)
        hg_ref[pl.ds(pl.multiple_of(half * 1024 + a * 256 + here * 64, 64), 64), cols] = (
            total.astype(BF))
        for i in (1, 3):
            second(half, h, 0, i, i)
            first(half, h, 0, 0, i, i)

    for h, half in both:
        on = 1 if h == 0 else 3
        for slot in (on, 4 - on):
            second_wait(half, h, slot)
            if slot == on:
                second(half, h, slot, on, 2)
            for i in (1, 3):
                first(half, h, slot, 0, i, i)

    def pass_on(h, half, j):
        on = 1 if h == 0 else 3
        first_wait(half, h, j, on)
        first(half, h, j, on, on, 2)

    for h, half in both:
        pass_on(h, half, 0)
    for h, half in both:
        second_wait(half, h, 2)
        for i in (1, 3):
            first(half, h, 2, 0, i, i)
    for j in (1, 3, 2):
        for h, half in both:
            pass_on(h, half, j)
    for h, half in both:
        on = 1 if h == 0 else 3
        for j in (0, 1, 3, 2):
            first_wait(half, h, j, 4 - on)
            first_wait(half, h, j, 2)
    finish()


def on_device(queries_in, head_weight, passages, teacher, cand_block, cand_offset, block_slot):
    vmem = pl.BlockSpec(memory_space=pltpu.VMEM)
    anywhere = pl.BlockSpec(memory_space=pl.ANY)
    V = pltpu.VMEM
    dma = pltpu.SemaphoreType.DMA
    kl, hg = pl.pallas_call(
        step_kernel,
        out_shape=(jax.ShapeDtypeStruct((1, 128), F32), pltpu.VMEM((2048, 1024), BF)),
        in_specs=[anywhere, anywhere, anywhere, vmem, vmem, vmem, vmem],
        out_specs=(vmem, vmem),
        scratch_shapes=[
            V((256, 2048), BF), V((2, 3, 256, 256), BF), V((2, 4, 256, 256), BF),
            V((2048, 1024), BF), V((1024, 1024), BF),
            V((128, 1024), F32), V((128, 1024), F32), V((128, 1024), F32), V((128, 1024), BF),
            V((ALL, 512), BF), V((4, 512, 192), BF), V((ALL, 128), BF), V((4, 128, 192), BF),
            V((4, 128, LANES), I32), V((128, LANES), I32),
            V((ALL, 1024), BF), V((ALL, 1024), BF), V((ALL, LANES), F32), V((ALL, LANES), F32),
            V((192, 384), BF), V((512, LANES), F32), V((4, 128, LANES), F32),
            V((ALL, LANES), BF), V((ALL, LANES), BF),
            V((ALL, 1024), BF), V((ALL, 1024), BF), V((ALL, 1024), BF),
            V((128, 1024), F32), V((256, 1024), BF), V((2, 3, 256, 1024), BF),
            V((2, 256, 1024), F32), V((2, 3, 64, 1024), BF), V((2, 3, 64, 1024), BF),
            dma((3,)), dma((5,)), dma((5,)), dma((4, 2, 16)), dma((4, 2, 16)),
            dma((4,)), dma((4,)),
            dma((2, 3)), dma((2, 3)), dma((2, 2, 3)), dma((2, 2, 3)), dma((2, 2, 3)),
            dma((2, 2, 3)), dma((2, 2, 3)), dma((2, 2, 3)), dma((2, 2, 3)), dma((2, 2, 3)),
            dma((2, 2, 4, 3)), dma((2, 2, 4, 3)),
        ],
        compiler_params=pltpu.CompilerParams(
            collective_id=0, has_side_effects=True, vmem_limit_bytes=VLIM),
    )(queries_in, head_weight, passages, teacher.reshape(128, 128).T,
      cand_offset.reshape(128, 128).T, cand_block.T, block_slot.reshape(1, 128))
    return kl.reshape(128), hg.astype(F32)


def solution(mesh):
    placed = (
        P(("corpus", "fsdp"), None),
        P("fsdp", "tensor"),
        P("corpus", "tensor"),
        P(("corpus", "fsdp"), None, None),
        P(("corpus", "fsdp"), None),
        P(("corpus", "fsdp"), None, None),
        P(),
    )
    return jax.shard_map(
        on_device,
        mesh=mesh,
        in_specs=placed,
        out_specs=(P(("corpus", "fsdp")), P("fsdp", "tensor")),
        check_vma=False,
    )
```

```python
import jax
import jax.numpy as jnp
from jax import lax
from jax.experimental import pallas as pl
from jax.experimental.pallas import tpu as pltpu
from jax.sharding import PartitionSpec as P

BF = jnp.bfloat16
F32 = jnp.float32
I32 = jnp.int32
SIDE = 4
SLOTS = 48
ALL = 768
LANES = 128
VLIM = 62_816_256
HALF = 512
MESH = pl.DeviceIdType.MESH
FAR = ((2, 2), (1, 2), (2, 1), (3, 2), (2, 3), (1, 1), (3, 3), (1, 3), (3, 1),
       (2, 0), (0, 2), (1, 0), (0, 1), (3, 0), (0, 3), (0, 0))


def dot(a, b, dims=((1,), (0,))):
    return lax.dot_general(a, b, (dims, ((), ())), preferred_element_type=F32)


def lane_pick(values, index):
    return jnp.take_along_axis(values, index, axis=1)


def step_kernel(x_hbm, w_hbm, p_hbm, teacher_ref, offs_ref, cand_ref, bslot_ref,
                kl_ref, hg_ref,
                xcat, xz, xzt, w, p, part_own, part_send, part_recv, q,
                pm, pmt, r, rtz, inv, offs_s,
                qs, qr, ss, sr, s3, dn, st, ds, dr, dexp, ps, pr, qga, qg2, qz,
                gown, hsend, hrecv,
                loc_sem, fs_send, fs_recv, aa_send, aa_recv, te_send, te_recv,
                xb_send, xb_recv, ql_send, ql_recv, qc_send, qc_recv,
                h_send, h_recv, s_send, s_recv, f_send, f_recv):
    c = lax.axis_index("corpus")
    f = lax.axis_index("fsdp")
    t = lax.axis_index("tensor")
    z = lax.div(c, SIDE)
    y = lax.rem(c, SIDE)
    sent = []
    looped = []

    def peer(dz, dy):
        return lax.rem(z + dz, SIDE) * SIDE + lax.rem(y + dy, SIDE)

    def source(dz, dy):
        return lax.rem(z + SIDE - dz, SIDE) * SIDE + lax.rem(y + SIDE - dy, SIDE)

    def half_cols(h):
        return pl.ds(h * HALF, HALF)

    own_cols = pl.ds(pl.multiple_of(f * 2048, 2048), 2048)
    other_cols = pl.ds(pl.multiple_of((1 - f) * 2048, 2048), 2048)
    load_x = pltpu.make_async_copy(
        x_hbm.at[:, own_cols], xcat.at[pl.ds(0, 128), :], loc_sem.at[0])
    load_w = [pltpu.make_async_copy(
        w_hbm.at[:, half_cols(h)], w.at[:, half_cols(h)], loc_sem.at[1 + h]) for h in range(2)]
    load_p = pltpu.make_async_copy(p_hbm, p, loc_sem.at[3])
    load_x.start()
    load_w[0].start()
    load_w[1].start()

    barrier = pltpu.get_barrier_semaphore()
    pl.semaphore_signal(barrier, inc=1, device_id={"fsdp": 1 - f}, device_id_type=MESH)

    @pl.loop(1, 4)
    def _(i):
        pl.semaphore_signal(
            barrier, inc=1, device_id={"tensor": lax.rem(t + i, 4)}, device_id_type=MESH)

    @pl.loop(1, 16)
    def _(i):
        pl.semaphore_signal(
            barrier, inc=1, device_id={"corpus": peer(lax.div(i, SIDE), lax.rem(i, SIDE))},
            device_id_type=MESH)

    lane = lax.broadcasted_iota(I32, (128, LANES), 1)
    row = lax.broadcasted_iota(I32, (128, LANES), 0)
    slot_of = jnp.broadcast_to(bslot_ref[...].astype(F32), (128, LANES)).T
    hits = jnp.zeros((128, LANES), F32)
    slots = []
    for g in range(4):
        named = cand_ref[g:g + 1, :] == row
        slot = jnp.sum(jnp.where(named, slot_of, 0.0), axis=0, keepdims=True).astype(I32)
        slots.append(slot)
        hits = hits + jnp.where(slot == row, 1.0, 0.0)
    earlier = jnp.where(row < lane, 1.0, 0.0).astype(BF)
    before = dot(hits.astype(BF), earlier)
    places = []
    for g in range(4):
        rank = jnp.sum(jnp.where(slots[g] == row, before, 0.0), axis=0, keepdims=True).astype(I32)
        places.append((slots[g] >> 3) * SLOTS + rank * 8 + (slots[g] & 7))
    for n in range(4):
        place_row = lax.broadcasted_iota(I32, (192, LANES), 0) + n * 192
        total = jnp.zeros((192, LANES), F32)
        for g in range(4):
            one = jnp.where(places[g] == place_row, 1.0, 0.0)
            total = total + one
            pm[n * 192:(n + 1) * 192, g * 128:(g + 1) * 128] = one.astype(BF)
        r[n * 192:(n + 1) * 192, :] = total.astype(BF)

    load_x.wait()
    for h in range(2):
        load_w[h].wait()
        if h == 1:
            load_p.start()

        @pl.loop(2 * h, 2 * h + 2)
        def _(n):
            cols = pl.ds(pl.multiple_of(n * 256, 256), 256)
            part_own[:, cols] = dot(xcat[0:128, :], w[:, cols])

    pl.semaphore_wait(barrier, 19)

    def fs_copy(src, dst, k):
        return pltpu.make_async_remote_copy(
            src_ref=src, dst_ref=dst, send_sem=fs_send.at[k], recv_sem=fs_recv.at[k],
            device_id={"fsdp": 1 - f}, device_id_type=MESH)

    def begin(copy):
        copy.start()
        sent.append(copy)
        return copy

    swap_x = begin(fs_copy(x_hbm.at[:, other_cols], xcat.at[pl.ds(128, 128), :], 0))

    def view(ref, at, h):
        rows = pl.ds(pl.multiple_of(at * SLOTS, 16), SLOTS)
        return ref.at[rows, :] if h is None else ref.at[rows, half_cols(h)]

    def out_copy(src, dst, chan, h, dz, dy):
        to, k, n = peer(dz, dy), 0 if h is None else h, dz * SIDE + dy
        return pltpu.make_async_remote_copy(
            src_ref=view(src, to, h), dst_ref=view(dst, c, h),
            send_sem=aa_send.at[chan, k, n], recv_sem=aa_recv.at[chan, k, n],
            device_id={"corpus": to}, device_id_type=MESH)

    def in_copy(src, dst, chan, h, dz, dy):
        frm, k, n = source(dz, dy), 0 if h is None else h, dz * SIDE + dy
        return pltpu.make_async_remote_copy(
            src_ref=view(src, frm, h), dst_ref=view(dst, frm, h),
            send_sem=aa_send.at[chan, k, n], recv_sem=aa_recv.at[chan, k, n],
            device_id={"corpus": frm}, device_id_type=MESH)

    def self_copy(src, dst, chan, h):
        return pltpu.make_async_copy(
            view(src, c, h), view(dst, c, h), aa_recv.at[chan, 0 if h is None else h, 0])

    def start_out(src, dst, chan, h, dz, dy):
        off = dz * SIDE + dy

        @pl.when(off == 0)
        def _():
            self_copy(src, dst, chan, h).start()

        @pl.when(off != 0)
        def _():
            out_copy(src, dst, chan, h, dz, dy).start()

    def wait_in(src, dst, chan, h, dz, dy):
        off = dz * SIDE + dy

        @pl.when(off == 0)
        def _():
            self_copy(src, dst, chan, h).wait()

        @pl.when(off != 0)
        def _():
            in_copy(src, dst, chan, h, dz, dy).wait_recv()

    def order(k):
        return (3 - k) ^ ((3 - k) >> 1)

    def wait_group(src, dst, chan, h, dz):
        @pl.loop(0, 4)
        def _(k):
            wait_in(src, dst, chan, h, dz, order(k))

    def group_rows(dz):
        zs = lax.rem(z + SIDE - dz, SIDE)
        return zs, pl.ds(pl.multiple_of(zs * 192, 16), 192)

    def answer_group(src, dst, chan, h, dz):
        @pl.loop(0, 4)
        def _(k):
            start_out(src, dst, chan, h, lax.rem(SIDE - dz, SIDE),
                      lax.rem(SIDE - order(k), SIDE))

    def finish():
        for copy in sent:
            copy.wait_send()
        for src, dst, chan, h in looped:
            @pl.loop(1, 16)
            def _(n, src=src, dst=dst, chan=chan, h=h):
                out_copy(src, dst, chan, h, lax.div(n, SIDE), lax.rem(n, SIDE)).wait_send()

    def along(half, stage, i):
        if (half == 0) == (stage == 0):
            there = lax.rem(z + i, SIDE)
            return there, there * SIDE + y
        there = lax.rem(y + i, SIDE)
        return there, z * SIDE + there

    def remote(src, dst, send_sem, recv_sem, dev):
        return pltpu.make_async_remote_copy(
            src_ref=src, dst_ref=dst, send_sem=send_sem, recv_sem=recv_sem,
            device_id={"corpus": dev}, device_id_type=MESH)

    def xb_copy(half, i, core):
        there, dev = along(half, 0, i)
        cols = pl.ds(pl.multiple_of(half * 1024 + there * 256, 256), 256)
        rows = pl.ds(core * 128, 128)
        return remote(xcat.at[rows, cols], xz.at[half, i - 1, rows, :],
                      xb_send.at[core, half, i - 1], xb_recv.at[core, half, i - 1], dev)

    for core in range(2):
        if core == 1:
            swap_x.wait_recv()
        for i in (2, 1, 3):
            for half in range(2):
                begin(xb_copy(half, i, core))

    swaps = []
    for h in range(2):
        @pl.loop(2 * h, 2 * h + 2)
        def _(n):
            cols = pl.ds(pl.multiple_of(n * 256, 256), 256)
            part_send[:, cols] = dot(xcat[128:256, :], w[:, cols])

        swaps.append(begin(fs_copy(
            part_send.at[:, half_cols(h)], part_recv.at[:, half_cols(h)], 1 + h)))

    for h in range(2):
        cols = half_cols(h)
        swaps[h].wait_recv()
        q[:, cols] = (part_own[:, cols] + part_recv[:, cols]).astype(BF)

        @pl.loop(0, 4)
        def _(n, cols=cols):
            rows = pl.ds(pl.multiple_of(n * 192, 16), 192)
            qs[rows, cols] = dot(r[rows, :], q[:, cols]).astype(BF)

        for dz, dy in FAR:
            if (dz, dy) == (0, 0):
                self_copy(qs, qr, 0, h).start()
            else:
                begin(out_copy(qs, qr, 0, h, dz, dy))

    offs = offs_ref[...].astype(F32).T.astype(I32)
    offs_s[...] = offs
    for g in range(4):
        inv[g, :, :] = jnp.full((128, LANES), -1, I32)

    @pl.loop(0, 32)
    def _(k):
        for g in range(4):
            at = jnp.full((128, LANES), g * 32, I32) + k
            here = lane_pick(offs_s[...], at)
            inv[g, :, :] = jnp.where(here == lane, at, inv[g, :, :])

    for n in range(4):
        rows = slice(n * 192, (n + 1) * 192)
        rtz[n, :, :] = r[rows, :].astype(F32).T.astype(BF)
        for g in range(4):
            pmt[n, g * 128:(g + 1) * 128, :] = (
                pm[rows, g * 128:(g + 1) * 128].astype(F32).T.astype(BF))
    dn[...] = jnp.zeros((512, LANES), F32)
    qga[...] = jnp.zeros((128, 1024), F32)

    load_p.wait()
    sub = lax.broadcasted_iota(I32, (192, LANES), 0) & 7
    for h in range(2):
        @pl.loop(0, 4)
        def _(k, h=h):
            dz = order(k)
            zs, rows = group_rows(dz)
            wait_group(qs, qr, 0, h, dz)
            acc = jnp.zeros((192, LANES), F32)
            for j in range(4):
                both = dot(qr[rows, half_cols(h)], p[j * 256:(j + 1) * 256, half_cols(h)],
                           ((1,), (1,)))
                acc = jnp.where(sub == 2 * j, both[:, :128], acc)
                acc = jnp.where(sub == 2 * j + 1, both[:, 128:], acc)
            if h == 0:
                ss[rows, :] = acc
            else:
                ss[rows, :] = ss[rows, :] + acc
                answer_group(ss, sr, 1, None, dz)
    looped.append((ss, sr, 1, None))

    @pl.loop(0, 4)
    def _(k):
        dz = order(k)
        zs, rows = group_rows(dz)
        wait_group(ss, sr, 1, None, dz)
        back = sr[rows, :]
        s3[:, 0:128] = back.astype(BF)
        back = back - s3[:, 0:128].astype(F32)
        s3[:, 128:256] = back.astype(BF)
        back = back - s3[:, 128:256].astype(F32)
        s3[:, 256:384] = back.astype(BF)
        three = dot(pmt[zs, :, :], s3[...])
        dn[...] = dn[...] + (three[:, 0:128] + (three[:, 128:256] + three[:, 256:384]))

    mine = jnp.zeros((128, LANES), F32)
    for g in range(4):
        mine = jnp.where((lane >> 5) == g,
                         lane_pick(dn[g * 128:(g + 1) * 128, :], offs_s[...]), mine)
    st[t, :, :] = mine

    def te_copy(i):
        return pltpu.make_async_remote_copy(
            src_ref=st.at[t], dst_ref=st.at[t],
            send_sem=te_send.at[i], recv_sem=te_recv.at[i],
            device_id={"tensor": lax.rem(t + i, 4)}, device_id_type=MESH)

    def te_in(i):
        frm = lax.rem(t + 4 - i, 4)
        return pltpu.make_async_remote_copy(
            src_ref=st.at[frm], dst_ref=st.at[frm],
            send_sem=te_send.at[i], recv_sem=te_recv.at[i],
            device_id={"tensor": frm}, device_id_type=MESH)

    for i in (2, 1, 3):
        begin(te_copy(i))
    teacher = teacher_ref[...].T
    teacher_top = jnp.max(teacher, axis=1, keepdims=True)
    teacher_lse = teacher_top + jnp.log(
        jnp.sum(jnp.exp(teacher - teacher_top), axis=1, keepdims=True))
    log_teacher = teacher - teacher_lse
    prob_teacher = jnp.exp(log_teacher)
    for i in (1, 3, 2):
        te_in(i).wait_recv()
    student = 50.0 * (((st[0, :, :] + st[1, :, :]) + st[2, :, :]) + st[3, :, :])
    top = jnp.max(student, axis=1, keepdims=True)
    log_student = student - (top + jnp.log(
        jnp.sum(jnp.exp(student - top), axis=1, keepdims=True)))
    dscore = (50.0 * (jnp.exp(log_student) - prob_teacher)).astype(BF).astype(F32)
    for g in range(4):
        at = inv[g, :, :]
        dense = jnp.where(at >= 0, lane_pick(dscore, jnp.maximum(at, 0)), 0.0)
        dexp[g * 128:(g + 1) * 128, 0:128] = dense.astype(BF)

    @pl.loop(0, 4)
    def _(k):
        dz = lax.rem(SIDE - order(k), SIDE)
        zs, rows = group_rows(dz)
        ds[rows, :] = dot(pm[rows, :], dexp[0:512, 0:128]).astype(BF)
        answer_group(ds, dr, 2, None, dz)
    looped.append((ds, dr, 2, None))

    terms = prob_teacher * (log_teacher - log_student)
    kl_ref[...] = jnp.sum(terms.T, axis=0, keepdims=True)

    for h in range(2):
        @pl.loop(0, 4)
        def _(k, h=h):
            dz = order(k)
            zs, rows = group_rows(dz)
            if h == 0:
                wait_group(ds, dr, 2, None, dz)
                given = dr[rows, :].astype(F32)
                for j in range(8):
                    dexp[rows, j * 128:(j + 1) * 128] = jnp.where(sub == j, given, 0.0).astype(BF)

            @pl.loop(2 * h, 2 * h + 2)
            def _(n):
                cols = pl.ds(pl.multiple_of(n * 256, 256), 256)
                ps[rows, cols] = dot(dexp[rows, :], p[:, cols]).astype(BF)

            answer_group(ps, pr, 3, h, dz)
        looped.append((ps, pr, 3, h))

    def wait_recv(dst, send_sem, recv_sem):
        remote(dst, dst, send_sem, recv_sem, lax.rem(c + 1, 16)).wait_recv()

    for half in range(2):
        here, _ = along(half, 0, 0)
        cols = pl.ds(pl.multiple_of(half * 1024 + here * 256, 256), 256)
        xzt[half, 0, :, :] = xcat[:, cols].T
        for i in (1, 3, 2):
            for core in range(2):
                wait_recv(xz.at[half, i - 1, pl.ds(core * 128, 128), :],
                          xb_send.at[core, half, i - 1], xb_recv.at[core, half, i - 1])
            xzt[half, i, :, :] = xz[half, i - 1, :, :].T

    def ql_copy(src, axis, h, i, slot):
        _, dev = along(axis, 0, i)
        return remote(src, qz.at[axis, slot - 1, pl.ds(0, 128), half_cols(h)],
                      ql_send.at[axis, h, slot - 1], ql_recv.at[axis, h, slot - 1], dev)

    def ql_wait(axis, h, slot):
        wait_recv(qz.at[axis, slot - 1, pl.ds(0, 128), half_cols(h)],
                  ql_send.at[axis, h, slot - 1], ql_recv.at[axis, h, slot - 1])

    def qc_copy(axis, h, slot):
        return pltpu.make_async_remote_copy(
            src_ref=qz.at[axis, slot - 1, pl.ds(0, 128), half_cols(h)],
            dst_ref=qz.at[axis, slot - 1, pl.ds(128, 128), half_cols(h)],
            send_sem=qc_send.at[axis, h, slot - 1], recv_sem=qc_recv.at[axis, h, slot - 1],
            device_id={"fsdp": 1 - f}, device_id_type=MESH)

    swap_q = []
    for h in range(2):
        cols = half_cols(h)

        @pl.loop(0, 4)
        def _(k, h=h, cols=cols):
            dz = order(k)
            zs, rows = group_rows(dz)
            wait_group(ps, pr, 3, h, dz)
            qga[:, cols] = qga[:, cols] + dot(rtz[zs, :, :], pr[rows, cols])

        qg2[0:128, cols] = qga[:, cols].astype(BF)
        mine = qg2.at[pl.ds(0, 128), cols]
        for i, slot in ((1, 1), (3, 3)):
            for axis in range(2):
                begin(ql_copy(mine, axis, h, i, slot))
        swap_q.append(begin(fs_copy(mine, qg2.at[pl.ds(128, 128), cols], 3 + h)))

    for h in range(2):
        on = 1 if h == 0 else 3
        for slot in (on, 4 - on):
            for axis in range(2):
                ql_wait(axis, h, slot)
                if slot == on:
                    begin(ql_copy(qz.at[axis, slot - 1, pl.ds(0, 128), half_cols(h)],
                                  axis, h, on, 2))
                begin(qc_copy(axis, h, slot))

    for h in range(2):
        cols = half_cols(h)
        swap_q[h].wait_recv()
        for half in range(2):
            gown[half, :, cols] = dot(xzt[half, 0, :, :], qg2[:, cols])
        for slot in (1, 3):
            for half in range(2):
                qc_copy(half, h, slot).wait_recv()
                gown[half, :, cols] = gown[half, :, cols] + dot(
                    xzt[half, slot, :, :], qz[half, slot - 1, :, cols])
        for half in range(2):
            ql_wait(half, h, 2)
            begin(qc_copy(half, h, 2))
        for half in range(2):
            qc_copy(half, h, 2).wait_recv()
            gown[half, :, cols] = gown[half, :, cols] + dot(
                xzt[half, 2, :, :], qz[half, 1, :, cols])
            for i in (2, 1, 3):
                there, dev = along(half, 1, i)
                rows = pl.ds(pl.multiple_of(there * 64, 64), 64)
                hsend[half, i - 1, :, cols] = gown[half, rows, cols].astype(BF)
                begin(remote(hsend.at[half, i - 1, :, cols], hrecv.at[half, i - 1, :, cols],
                             h_send.at[half, h, i - 1], h_recv.at[half, h, i - 1], dev))

    def piece(half, h, i, j):
        a, _ = along(half, 0, SIDE - i)
        b, _ = along(half, 1, SIDE - j)
        rows = pl.ds(pl.multiple_of(half * 1024 + a * 256 + b * 64, 64), 64)
        return hg_ref.at[rows, half_cols(h)]

    def second(half, h, j, i, slot):
        ref = piece(half, h, 0, j)
        _, dev = along(half, 1, i)
        begin(remote(ref, ref, s_send.at[half, h, slot - 1], s_recv.at[half, h, slot - 1], dev))

    def second_wait(half, h, slot):
        wait_recv(piece(half, h, 0, slot), s_send.at[half, h, slot - 1],
                  s_recv.at[half, h, slot - 1])

    def first(half, h, j, k, i, slot):
        ref = piece(half, h, k, j)
        _, dev = along(half, 0, i)
        begin(remote(ref, ref, f_send.at[half, h, j, slot - 1],
                     f_recv.at[half, h, j, slot - 1], dev))

    def first_wait(half, h, j, slot):
        wait_recv(piece(half, h, slot, j), f_send.at[half, h, j, slot - 1],
                  f_recv.at[half, h, j, slot - 1])

    both = [(h, half) for h in range(2) for half in range(2)]
    for h, half in both:
        cols = half_cols(h)
        for i in (1, 3, 2):
            wait_recv(hrecv.at[half, i - 1, :, cols], h_send.at[half, h, i - 1],
                      h_recv.at[half, h, i - 1])
        here, _ = along(half, 1, 0)
        total = gown[half, pl.ds(pl.multiple_of(here * 64, 64), 64), cols]
        for i in (1, 2, 3):
            total = total + hrecv[half, i - 1, :, cols].astype(F32)
        a, _ = along(half, 0, 0)
        hg_ref[pl.ds(pl.multiple_of(half * 1024 + a * 256 + here * 64, 64), 64), cols] = (
            total.astype(BF))
        for i in (1, 3):
            second(half, h, 0, i, i)
            first(half, h, 0, 0, i, i)

    for h, half in both:
        on = 1 if h == 0 else 3
        for slot in (on, 4 - on):
            second_wait(half, h, slot)
            if slot == on:
                second(half, h, slot, on, 2)
            for i in (1, 3):
                first(half, h, slot, 0, i, i)

    def pass_on(h, half, j):
        on = 1 if h == 0 else 3
        first_wait(half, h, j, on)
        first(half, h, j, on, on, 2)

    for h, half in both:
        pass_on(h, half, 0)
    for h, half in both:
        second_wait(half, h, 2)
        for i in (1, 3):
            first(half, h, 2, 0, i, i)
    for j in (1, 3, 2):
        for h, half in both:
            pass_on(h, half, j)
    for h, half in both:
        on = 1 if h == 0 else 3
        for j in (0, 1, 3, 2):
            first_wait(half, h, j, 4 - on)
            first_wait(half, h, j, 2)
    finish()


def on_device(queries_in, head_weight, passages, teacher, cand_block, cand_offset, block_slot):
    vmem = pl.BlockSpec(memory_space=pltpu.VMEM)
    anywhere = pl.BlockSpec(memory_space=pl.ANY)
    V = pltpu.VMEM
    dma = pltpu.SemaphoreType.DMA
    kl, hg = pl.pallas_call(
        step_kernel,
        out_shape=(jax.ShapeDtypeStruct((1, 128), F32), pltpu.VMEM((2048, 1024), BF)),
        in_specs=[anywhere, anywhere, anywhere, vmem, vmem, vmem, vmem],
        out_specs=(vmem, vmem),
        scratch_shapes=[
            V((256, 2048), BF), V((2, 3, 256, 256), BF), V((2, 4, 256, 256), BF),
            V((2048, 1024), BF), V((1024, 1024), BF),
            V((128, 1024), F32), V((128, 1024), F32), V((128, 1024), F32), V((128, 1024), BF),
            V((ALL, 512), BF), V((4, 512, 192), BF), V((ALL, 128), BF), V((4, 128, 192), BF),
            V((4, 128, LANES), I32), V((128, LANES), I32),
            V((ALL, 1024), BF), V((ALL, 1024), BF), V((ALL, LANES), F32), V((ALL, LANES), F32),
            V((192, 384), BF), V((512, LANES), F32), V((4, 128, LANES), F32),
            V((ALL, LANES), BF), V((ALL, LANES), BF),
            V((ALL, 1024), BF), V((ALL, 1024), BF), V((ALL, 1024), BF),
            V((128, 1024), F32), V((256, 1024), BF), V((2, 3, 256, 1024), BF),
            V((2, 256, 1024), F32), V((2, 3, 64, 1024), BF), V((2, 3, 64, 1024), BF),
            dma((4,)), dma((5,)), dma((5,)), dma((4, 2, 16)), dma((4, 2, 16)),
            dma((4,)), dma((4,)),
            dma((2, 2, 3)), dma((2, 2, 3)), dma((2, 2, 3)), dma((2, 2, 3)), dma((2, 2, 3)),
            dma((2, 2, 3)), dma((2, 2, 3)), dma((2, 2, 3)), dma((2, 2, 3)), dma((2, 2, 3)),
            dma((2, 2, 4, 3)), dma((2, 2, 4, 3)),
        ],
        compiler_params=pltpu.CompilerParams(
            collective_id=0, has_side_effects=True, vmem_limit_bytes=VLIM),
    )(queries_in, head_weight, passages, teacher.reshape(128, 128).T,
      cand_offset.reshape(128, 128).T, cand_block.T, block_slot.reshape(1, 128))
    return kl.reshape(128), hg.astype(F32)


def solution(mesh):
    placed = (
        P(("corpus", "fsdp"), None),
        P("fsdp", "tensor"),
        P("corpus", "tensor"),
        P(("corpus", "fsdp"), None, None),
        P(("corpus", "fsdp"), None),
        P(("corpus", "fsdp"), None, None),
        P(),
    )
    return jax.shard_map(
        on_device,
        mesh=mesh,
        in_specs=placed,
        out_specs=(P(("corpus", "fsdp")), P("fsdp", "tensor")),
        check_vma=False,
    )
```
